256 devices in a mesh: dp: 8 (over x, core), shard: 32 (over y, z).
Axes of the slice: x: 4, y: 4, z: 8, core: 2. Of those that a mesh axis runs over, the one named last changes fastest.
Arguments:
- queries: bfloat16 [2048, 256], P(('dp', 'shard')), may hold values from -1 to 1
- query_labels: int32 [2048], P(('dp', 'shard')), may hold values from 0 to 511, as said below
- positive_ids: int32 [2048, 64], P(('dp', 'shard')), may hold values from 0 to 32767, as said below
- positive_mask: int32 [2048, 64], P(('dp', 'shard')), may hold values from 0 to 1, as said below
- memory: bfloat16 [32768, 256], P('shard'), may hold values from -1 to 1
- memory_labels: int32 [32768], P('shard'), may hold values from 0 to 511
Outputs:
- precision: float32 [2048], P(('dp', 'shard'))
- query_grad: float32 [2048, 256], P(('dp', 'shard'))
The draws below stay inside these ranges and needn't reach their ends.
Inputs may be any that keep to these rules, and one draw needn't show every extreme that they name: `positive_ids`: each query's used slots come first; they name distinct memory rows whose label equals the query's label, as many as min(64, rows of that class); unused slots hold 0. `positive_mask`: the first slot of every query is used. `query_labels`: every query's label is the label of some memory row.
All inputs are finite; a program needn't handle non-finite values.
Results may differ from the reference program's by a relative error of at most 0.0014.
Values may be sent and summed in bfloat16 or wider, within the bound.
A program may use at most 64 MiB of HBM per device.

```python
import jax
import jax.numpy as jnp
from jax import lax

D = 256
POS = 64
QGROUP = 256
Q_TOTAL = 2048
R_TOTAL = 32768
CLASSES = 512


def integer_tables(key):
    base = jax.random.fold_in(key, 7001)
    key_one, key_two, key_three, key_four = jax.random.split(base, 4)
    first_pick = jax.random.randint(key_one, (R_TOTAL,), 0, CLASSES).astype(jnp.int32)
    second_pick = jax.random.randint(key_four, (R_TOTAL,), 0, CLASSES).astype(jnp.int32)
    row_index = jnp.arange(R_TOTAL, dtype=jnp.int32)
    mem_labels = jnp.where(row_index == R_TOTAL - 1, CLASSES - 1, jnp.minimum(first_pick, second_pick)).astype(jnp.int32)
    shuffle = jax.random.permutation(key_three, R_TOTAL).astype(jnp.int32)
    order = jnp.argsort(mem_labels * R_TOTAL + shuffle, stable=True).astype(jnp.int32)
    picked = jax.random.randint(key_two, (Q_TOTAL,), 0, R_TOTAL).astype(jnp.int32)
    query_index = jnp.arange(Q_TOTAL, dtype=jnp.int32)
    picked = jnp.where(query_index == 0, order[0], picked)
    picked = jnp.where(query_index == Q_TOTAL - 1, R_TOTAL - 1, picked).astype(jnp.int32)
    q_labels = mem_labels[picked]
    counts = jax.ops.segment_sum(jnp.ones((R_TOTAL,), jnp.int32), mem_labels, CLASSES)
    starts = jnp.cumsum(counts) - counts
    slots = jnp.arange(POS, dtype=jnp.int32)
    have = counts[q_labels]
    first_row = starts[q_labels]
    valid = slots[None, :] < have[:, None]
    where_in = first_row[:, None] + jnp.minimum(slots[None, :], jnp.maximum(have[:, None] - 1, 0))
    ids = jnp.where(valid, order[where_in], 0).astype(jnp.int32)
    sorted_labels = mem_labels[order]
    place = jnp.arange(R_TOTAL, dtype=jnp.int32) - starts[sorted_labels]
    spare_sorted = place >= POS
    spare_rank = jnp.cumsum(spare_sorted.astype(jnp.int32)) - 1
    target_sorted = jnp.where(spare_sorted, spare_rank % Q_TOTAL, 0).astype(jnp.int32)
    spare = jnp.zeros((R_TOTAL,), jnp.bool_).at[order].set(spare_sorted)
    target = jnp.zeros((R_TOTAL,), jnp.int32).at[order].set(target_sorted)
    planted = spare & (q_labels[target] != mem_labels)
    return (mem_labels, q_labels, ids, valid.astype(jnp.int32), planted, target)


def float_tables(key):
    mem_labels, q_labels, ids, valid, planted, target = integer_tables(key)
    base = jax.random.fold_in(key, 9103)
    keys = jax.random.split(base, 6)
    center_std = (7.0 / D) ** 0.5
    noise_std = D ** (-0.5)
    centers = jax.random.normal(keys[0], (CLASSES, D), jnp.float32) * center_std
    row_scale = jnp.exp(jax.random.uniform(keys[2], (R_TOTAL, 1), jnp.float32, jnp.log(0.8), jnp.log(1.6)))
    mem_base = centers[mem_labels] * row_scale + jax.random.normal(keys[1], (R_TOTAL, D), jnp.float32) * noise_std
    q_noise = jax.random.normal(keys[3], (Q_TOTAL, D), jnp.float32) * noise_std
    queries = jnp.clip(centers[q_labels] + q_noise, -1.0, 1.0)
    base_clipped = jnp.clip(mem_base, -1.0, 1.0)
    base_rounded = base_clipped.astype(jnp.bfloat16)
    query_rounded = queries.astype(jnp.bfloat16)

    def lowest(item):
        row, slots, used = item
        scored = jnp.dot(base_rounded[slots], row, preferred_element_type=jnp.float32)
        return jnp.min(jnp.where(used > 0, scored, 1000000000.0))
    low = lax.map(lowest, (query_rounded, ids, valid))
    query_wide = query_rounded.astype(jnp.float32)
    aimed = query_wide[target]
    length = jnp.sum(aimed * aimed, axis=1, keepdims=True)
    gap = jax.random.uniform(keys[4], (R_TOTAL, 1), jnp.float32, 0.305, 0.345)
    spread = jax.random.normal(keys[5], (R_TOTAL, D), jnp.float32) * noise_std
    spread = spread - jnp.sum(spread * aimed, axis=1, keepdims=True) / length * aimed
    placed = (low[target][:, None] - gap) / length * aimed + spread
    memory = jnp.where(planted[:, None], jnp.clip(placed, -1.0, 1.0), base_clipped)
    return (queries, memory)


def draw_queries(key, part):
    return float_tables(key)[0].astype(jnp.bfloat16)


def draw_memory(key, part):
    return float_tables(key)[1].astype(jnp.bfloat16)


def draw_memory_labels(key, part):
    return integer_tables(key)[0]


def draw_query_labels(key, part):
    return integer_tables(key)[1]


def draw_positive_ids(key, part):
    return integer_tables(key)[2]


def draw_positive_mask(key, part):
    return integer_tables(key)[3]


def setup_inputs(seed: int = 0) -> dict:
    key_list = jax.random.split(jax.random.key(seed), 7)
    queries = draw_queries(jax.random.fold_in(key_list[6], 71), 0)
    query_labels = draw_query_labels(jax.random.fold_in(key_list[6], 71), 0)
    positive_ids = draw_positive_ids(jax.random.fold_in(key_list[6], 71), 0)
    positive_mask = draw_positive_mask(jax.random.fold_in(key_list[6], 71), 0)
    memory = draw_memory(jax.random.fold_in(key_list[6], 71), 0)
    memory_labels = draw_memory_labels(jax.random.fold_in(key_list[6], 71), 0)
    return {"queries": queries, "query_labels": query_labels, "positive_ids": positive_ids, "positive_mask": positive_mask, "memory": memory, "memory_labels": memory_labels}


TAU = 0.1


def positive_terms(positive, mask, rank_neg, slope_neg):
    maskf = mask.astype(jnp.float32)
    count = positive.shape[1]
    diff = (positive[:, None, :] - positive[:, :, None]) / TAU
    sig = jax.nn.sigmoid(diff)
    off = 1.0 - jnp.eye(count, dtype=jnp.float32)
    live = maskf[:, None, :] * off[None]
    rank_pos = 1.0 + jnp.sum(live * sig, axis=2)
    total = rank_pos + rank_neg
    found = jnp.sum(maskf, axis=1)
    precision = jnp.sum(maskf * rank_pos / total, axis=1) / found
    weight_neg = maskf * rank_pos / (found[:, None] * total * total)
    weight_pos = -maskf * rank_neg / (found[:, None] * total * total)
    slope = sig * (1.0 - sig) * off[None]
    spread = jnp.sum(maskf[:, None, :] * slope, axis=2)
    backed = jnp.sum(weight_pos[:, None, :] * slope, axis=2)
    dpos = (-weight_neg * slope_neg - weight_pos * spread + maskf * backed) / TAU
    return precision, weight_neg, dpos


def reference(queries, query_labels, positive_ids, positive_mask, memory, memory_labels):
    width = queries.shape[1]
    count = positive_ids.shape[1]
    mem_wide = memory.astype(jnp.float32)

    def one_group(items):
        group_q, labels, ids, mask = items
        scores = jnp.dot(group_q, memory.T, preferred_element_type=jnp.float32)
        positive = jnp.take_along_axis(scores, ids, axis=1)
        negative = memory_labels[None, :] != labels[:, None]

        def first(carry, column):
            sig = jax.nn.sigmoid((scores - column[:, None]) / TAU)
            kept = jnp.where(negative, sig, 0.0)
            return carry, (jnp.sum(kept, axis=1), jnp.sum(kept * (1.0 - sig), axis=1))

        _, (rank_neg, slope_neg) = lax.scan(first, jnp.zeros((), jnp.float32), positive.T)
        precision, weight_neg, dpos = positive_terms(positive, mask, rank_neg.T, slope_neg.T)

        def second(acc, pair):
            column, weight = pair
            sig = jax.nn.sigmoid((scores - column[:, None]) / TAU)
            return acc + weight[:, None] * sig * (1.0 - sig), None

        neg_acc, _ = lax.scan(second, jnp.zeros(scores.shape, jnp.float32), (positive.T, weight_neg.T))
        rows = jnp.arange(group_q.shape[0], dtype=jnp.int32)[:, None]
        pos_acc = jnp.zeros(scores.shape, jnp.float32).at[rows, ids].add(dpos)
        cotangent = jnp.where(negative, neg_acc / TAU, 0.0) + pos_acc
        grad = jnp.dot(cotangent, mem_wide, precision=lax.Precision.HIGHEST, preferred_element_type=jnp.float32)
        return precision, grad

    groups = queries.shape[0] // QGROUP
    items = (queries.reshape(groups, QGROUP, width), query_labels.reshape(groups, QGROUP),
             positive_ids.reshape(groups, QGROUP, count), positive_mask.reshape(groups, QGROUP, count))
    precision, grad = lax.map(one_group, items)
    return precision.reshape(-1), grad.reshape(-1, width)
```

```python
import functools

import jax
import jax.numpy as jnp
from jax import lax
from jax.experimental import pallas as pl
from jax.experimental.pallas import tpu as pltpu
from jax.sharding import PartitionSpec as P

F32 = jnp.float32
BF16 = jnp.bfloat16
I32 = jnp.int32
HALF_INV_TAU = 5.0
FAR = -1e6
MESH = pl.DeviceIdType.MESH
G = 8
KB = 4
JB = 16


def dot_nt(a, b):
    return lax.dot_general(a, b, (((1,), (1,)), ((), ())), preferred_element_type=F32)


def dot_nn(a, b):
    return lax.dot_general(a, b, (((1,), (0,)), ((), ())), preferred_element_type=F32)


def lane_gather(table, index):
    return jnp.take_along_axis(table, index, axis=1, mode="promise_in_bounds")


def kernel(
    n, q_ref, tab_ref, mem_ref, mlab_ref, prec_ref, grad_ref,
    qall, idall, s_ref, st_ref, inv_ref, ct_ref,
    ppart, prs, pown, pall, pt_ref, wq_ref, aux_ref,
    rsum, rpart, rrs, wdown, wdall, wdt_ref, gpart, grs,
    send_sem, recv_sem,
):
    me = lax.axis_index("shard")
    rows = mem_ref.shape[0]
    base = me * rows
    nb = rows // 128
    nh = n // 2
    my_half = me // nh

    def peer_of(d):
        return lax.rem(me + d, n)

    barrier = pltpu.get_barrier_semaphore()

    def greet(d, c):
        pl.semaphore_signal(barrier, inc=1, device_id={"shard": peer_of(d)}, device_id_type=MESH)
        return c

    lax.fori_loop(1, n, greet, 0)
    qall[me] = q_ref[...]
    idall[me] = tab_ref[...]
    pl.semaphore_wait(barrier, n - 1)

    def put(src, dst, phase, peer):
        pltpu.make_async_remote_copy(
            src_ref=src, dst_ref=dst, send_sem=send_sem.at[phase], recv_sem=recv_sem.at[phase],
            device_id={"shard": peer}, device_id_type=MESH,
        ).start()

    def await_blocks(sem, phase, buf, count):
        view = buf.at[pl.ds(0, count)]
        pltpu.make_async_copy(view, view, sem.at[phase]).wait()

    def spread_inputs(d, c):
        peer = peer_of(d)
        put(tab_ref, idall.at[me], 1, peer)
        put(q_ref, qall.at[me], 0, peer)
        return c

    lax.fori_loop(1, n, spread_inputs, 0)
    await_blocks(recv_sem, 1, idall, n - 1)
    await_blocks(recv_sem, 0, qall, n - 1)

    queries = qall[...].astype(F32).reshape(n * 8, q_ref.shape[1]).astype(BF16)
    mlab_t = jnp.transpose(jnp.concatenate([mlab_ref[...]] * 16, axis=0))
    id_t = [jnp.transpose(idall[pl.ds(h * nh, nh)].reshape(nh * 8, 128)) for h in range(2)]
    for a in range(nb):
        block = mem_ref[pl.ds(a * 128, 128), :]
        s_ref[:, pl.ds(a * 128, 128)] = dot_nt(queries, block)
        st = dot_nt(block, queries) * HALF_INV_TAU
        column = jnp.broadcast_to(mlab_t[:, a : a + 1], (128, 128))
        for h in range(2):
            label = id_t[h][64:65, :]
            st_ref[pl.ds(a * 128, 128), pl.ds(h * 128, 128)] = jnp.where(
                column != label, st[:, h * 128 : (h + 1) * 128], FAR
            )

    lane = lax.broadcasted_iota(I32, (8, 128), 1)

    def pick(b, c):
        local = idall[b] - base
        place = jnp.bitwise_and(local, 127)
        which = jnp.right_shift(local, 7)
        value = jnp.zeros((8, 128), F32)
        for a in range(nb):
            table = s_ref[pl.ds(pl.multiple_of(b * 8, 8), 8), pl.ds(a * 128, 128)]
            value = jnp.where(which == a, lane_gather(table, place), value)
        ppart[b] = jnp.where(lane < 64, value * HALF_INV_TAU, 0.0)
        return c

    lax.fori_loop(0, n, pick, 0)

    def send_positive(d, c):
        peer = peer_of(d)
        put(ppart.at[peer], prs.at[me], 2, peer)
        return c

    lax.fori_loop(1, n, send_positive, 0)
    prs[me] = ppart[me]
    await_blocks(recv_sem, 2, prs, n - 1)
    own = jnp.sum(prs[...], axis=0)
    pown[...] = own
    pall[me] = own

    def spread_positive(d, c):
        put(pown, pall.at[me], 3, peer_of(d))
        return c

    lax.fori_loop(1, n, spread_positive, 0)

    mask = jnp.where(jnp.logical_and(lane < 64, tab_ref[...] >= 0), 1.0, 0.0)
    own_t = jnp.transpose(jnp.concatenate([own] * 16, axis=0))
    mask_t = jnp.transpose(jnp.concatenate([mask] * 16, axis=0))
    off = jnp.where(
        lax.broadcasted_iota(I32, (64, 128), 0) == lax.broadcasted_iota(I32, (64, 128), 1), 0.0, 1.0
    )
    for i in range(8):
        col = jnp.broadcast_to(own_t[:64, i : i + 1], (64, 128))
        mcol = jnp.broadcast_to(mask_t[:64, i : i + 1], (64, 128)) * off
        t = jnp.tanh(col - own[i : i + 1, :])
        w = (1.0 - t * t) * (0.25 * off)
        wq_ref[i] = w
        aux_ref[i : i + 1, :] = 1.0 + jnp.sum(mcol * (0.5 + 0.5 * t), axis=0, keepdims=True)
        aux_ref[8 + i : 9 + i, :] = jnp.sum(mcol * w, axis=0, keepdims=True)

    def invert(b, c):
        local = idall[b] - base
        found = [jnp.full((8, 128), -1, I32) for _ in range(nb)]
        for k in range(64):
            here = jnp.broadcast_to(local[:, k : k + 1], (8, 128))
            for a in range(nb):
                found[a] = jnp.where(here == lane + a * 128, 64 + k, found[a])
        for a in range(nb):
            inv_ref[pl.ds(pl.multiple_of(b * 8, 8), 8), pl.ds(a * 128, 128)] = found[a]
        return c

    lax.fori_loop(0, n, invert, 0)

    await_blocks(recv_sem, 3, pall, n - 1)
    for h in range(2):
        pt_ref[h] = jnp.transpose(pall[pl.ds(h * nh, nh)].reshape(nh * 8, 128))[:64, :]

    def row_of(ref, k, h):
        return jnp.broadcast_to(ref[h, pl.ds(k, 1), :], (8, 128))

    def first_pass(h):
        def slots(kb, c):
            p = [row_of(pt_ref, kb * KB + i, h) for i in range(KB)]

            def step(g, acc):
                acc = list(acc)
                s = [
                    st_ref[pl.ds(pl.multiple_of(g * (8 * G), 8 * G) + 8 * v, 8), pl.ds(h * 128, 128)]
                    for v in range(G)
                ]
                for i in range(KB):
                    one = two = None
                    for v in range(G):
                        t = jnp.tanh(s[v] - p[i])
                        one = t if one is None else one + t
                        two = t * t if two is None else two + t * t
                    acc[2 * i] = acc[2 * i] + (one + float(G))
                    acc[2 * i + 1] = acc[2 * i + 1] + (float(G) - two)
                return tuple(acc)

            zero = jnp.zeros((8, 128), F32)
            acc = lax.fori_loop(0, rows // (8 * G), step, (zero,) * (2 * KB))
            for i in range(KB):
                rsum[pl.ds(kb * KB + i, 1), :] = 0.5 * jnp.sum(acc[2 * i], axis=0, keepdims=True)
                rsum[pl.ds(64 + kb * KB + i, 1), :] = 0.25 * jnp.sum(
                    acc[2 * i + 1], axis=0, keepdims=True
                )
            return c

        lax.fori_loop(0, 64 // KB, slots, 0)
        rpart[pl.ds(h * nh, nh)] = jnp.transpose(rsum[...]).reshape(nh, 8, 128)

        def send(d, c):
            owner = h * nh + lax.rem(me + d, nh)

            @pl.when(owner != me)
            def _():
                put(rpart.at[owner], rrs.at[me], 4 + h, owner)

            return c

        lax.fori_loop(0, nh, send, 0)

    def owner_terms(h):
        rrs[me] = rpart[me]
        await_blocks(recv_sem, 4 + h, rrs, n - 1)
        both = jnp.sum(rrs[...], axis=0)
        slope_neg = pltpu.roll(both, 64, axis=1)
        rank_neg = both
        rank_pos = aux_ref[0:8, :]
        spread = aux_ref[8:16, :]
        total = rank_pos + rank_neg
        found = jnp.sum(mask, axis=1, keepdims=True)
        share = mask / (found * total * total)
        weight_neg = share * rank_pos
        weight_pos = -share * rank_neg
        precision = jnp.sum(mask * rank_pos / total, axis=1, keepdims=True) / found
        prec_ref[...] = jnp.broadcast_to(precision, (8, 128))
        wp_t = jnp.transpose(jnp.concatenate([weight_pos] * 16, axis=0))
        for i in range(8):
            col = jnp.broadcast_to(wp_t[:64, i : i + 1], (64, 128))
            aux_ref[16 + i : 17 + i, :] = jnp.sum(col * wq_ref[i], axis=0, keepdims=True)
        backed = aux_ref[16:24, :]
        dpos = (mask * backed - weight_neg * slope_neg - weight_pos * spread) * (2.0 * HALF_INV_TAU)
        both = jnp.where(lane < 64, weight_neg * (0.5 * HALF_INV_TAU), pltpu.roll(dpos, 64, axis=1))
        wdown[...] = both
        wdall[me] = both

        def spread_weights(d, c):
            put(wdown, wdall.at[me], 6 + h, peer_of(d))
            return c

        lax.fori_loop(1, n, spread_weights, 0)

    def second_pass(h):
        @pl.when(my_half == h)
        def _():
            await_blocks(recv_sem, 6 + h, wdall, nh - 1)

        @pl.when(my_half != h)
        def _():
            await_blocks(recv_sem, 6 + h, wdall, nh)

        wdt_ref[h] = jnp.transpose(wdall[pl.ds(h * nh, nh)].reshape(nh * 8, 128))

        def block(jb, c):
            start = pl.multiple_of(jb * (8 * JB), 8 * JB)
            s = [st_ref[pl.ds(start + 8 * v, 8), pl.ds(h * 128, 128)] for v in range(JB)]

            def slot(k, acc):
                p = row_of(pt_ref, k, h)
                w = row_of(wdt_ref, k, h)
                out = []
                for v in range(JB):
                    t = jnp.tanh(s[v] - p)
                    out.append(acc[v] + w * (1.0 - t * t))
                return tuple(out)

            zero = jnp.zeros((8, 128), F32)
            acc = lax.fori_loop(0, 64, slot, (zero,) * JB, unroll=2)
            for v in range(JB):
                ct_ref[pl.ds(start + 8 * v, 8), :] = acc[v]
            return c

        lax.fori_loop(0, rows // (8 * JB), block, 0)
        hi, lo = [], []
        for a in range(nb):
            neg = jnp.transpose(ct_ref[pl.ds(a * 128, 128), :])
            pos = []
            for b in range(nh):
                index = inv_ref[pl.ds((h * nh + b) * 8, 8), pl.ds(a * 128, 128)]
                value = lane_gather(wdall[h * nh + b], jnp.bitwise_and(index, 127))
                pos.append(jnp.where(index >= 0, value, 0.0))
            cot = neg + jnp.concatenate(pos, axis=0)
            top = cot.astype(BF16)
            hi.append(top)
            lo.append((cot - top.astype(F32)).astype(BF16))
        memory = mem_ref[...]
        grad = dot_nn(jnp.concatenate(hi, axis=1), memory) + dot_nn(
            jnp.concatenate(lo, axis=1), memory
        )
        gpart[pl.ds(h * nh, nh)] = grad.reshape(nh, 8, grad.shape[1])

        def send(d, c):
            owner = h * nh + lax.rem(me + d, nh)

            @pl.when(owner != me)
            def _():
                put(gpart.at[owner], grs.at[me], 8 + h, owner)

            return c

        lax.fori_loop(0, nh, send, 0)

    first_pass(0)
    first_pass(1)
    for h in range(2):
        pl.when(my_half == h)(functools.partial(owner_terms, h))
    second_pass(0)
    second_pass(1)

    grs[me] = gpart[me]
    for h in range(2):
        @pl.when(my_half == h)
        def _():
            await_blocks(recv_sem, 8 + h, grs, n - 1)
            await_blocks(send_sem, 4 + h, rpart, nh - 1)
            await_blocks(send_sem, 5 - h, rpart, nh)
            await_blocks(send_sem, 8 + h, gpart, nh - 1)
            await_blocks(send_sem, 9 - h, gpart, nh)
            await_blocks(send_sem, 6 + h, wdall, n - 1)

    grad_ref[...] = jnp.sum(grs[...], axis=0)
    await_blocks(send_sem, 0, qall, n - 1)
    await_blocks(send_sem, 1, idall, n - 1)
    await_blocks(send_sem, 2, ppart, n - 1)
    await_blocks(send_sem, 3, pall, n - 1)


def on_device(n, queries, query_labels, positive_ids, positive_mask, memory, memory_labels):
    own, width = queries.shape
    rows = memory.shape[0]
    slots = positive_ids.shape[1]
    table = jnp.concatenate(
        [
            jnp.where(positive_mask > 0, positive_ids, -1),
            jnp.broadcast_to(query_labels[:, None], (own, slots)),
        ],
        axis=1,
    )
    vmem = pl.BlockSpec(memory_space=pltpu.VMEM)
    nq = n * own
    precision, grad = pl.pallas_call(
        functools.partial(kernel, n),
        out_shape=(
            jax.ShapeDtypeStruct((own, 128), F32),
            jax.ShapeDtypeStruct((own, width), F32),
        ),
        in_specs=[vmem] * 4,
        out_specs=(vmem, vmem),
        scratch_shapes=[
            pltpu.VMEM((n, own, width), BF16),
            pltpu.VMEM((n, own, 128), I32),
            pltpu.VMEM((nq, rows), F32),
            pltpu.VMEM((rows, nq), F32),
            pltpu.VMEM((nq, rows), I32),
            pltpu.VMEM((rows, 128), F32),
            pltpu.VMEM((n, own, 128), F32),
            pltpu.VMEM((n, own, 128), F32),
            pltpu.VMEM((own, 128), F32),
            pltpu.VMEM((n, own, 128), F32),
            pltpu.VMEM((2, slots, 128), F32),
            pltpu.VMEM((own, slots, 128), F32),
            pltpu.VMEM((24, 128), F32),
            pltpu.VMEM((128, 128), F32),
            pltpu.VMEM((n, own, 128), F32),
            pltpu.VMEM((n, own, 128), F32),
            pltpu.VMEM((own, 128), F32),
            pltpu.VMEM((n, own, 128), F32),
            pltpu.VMEM((2, 128, 128), F32),
            pltpu.VMEM((n, own, width), F32),
            pltpu.VMEM((n, own, width), F32),
            pltpu.SemaphoreType.DMA((10,)),
            pltpu.SemaphoreType.DMA((10,)),
        ],
        compiler_params=pltpu.CompilerParams(collective_id=0, has_side_effects=True),
    )(queries, table, memory, memory_labels.reshape(rows // 128, 128))
    return precision[:, 0], grad


def solution(mesh):
    n = mesh.shape["shard"]
    return jax.shard_map(
        functools.partial(on_device, n),
        mesh=mesh,
        in_specs=(
            P(("dp", "shard"), None),
            P(("dp", "shard")),
            P(("dp", "shard"), None),
            P(("dp", "shard"), None),
            P("shard", None),
            P("shard"),
        ),
        out_specs=(P(("dp", "shard")), P(("dp", "shard"), None)),
        check_vma=False,
    )
```

```python
import functools

import jax
import jax.numpy as jnp
from jax import lax
from jax.experimental import pallas as pl
from jax.experimental.pallas import tpu as pltpu
from jax.sharding import PartitionSpec as P

F32 = jnp.float32
BF16 = jnp.bfloat16
I32 = jnp.int32
HALF_INV_TAU = 5.0
FAR = -1e6
MESH = pl.DeviceIdType.MESH
G = 8
KB = 4
JB = 8
NY, NZ = 4, 8
NC, NO = 4, 8
SPLIT = 12


def dot_nt(a, b):
    return lax.dot_general(a, b, (((1,), (1,)), ((), ())), preferred_element_type=F32)


def dot_nn(a, b):
    return lax.dot_general(a, b, (((1,), (0,)), ((), ())), preferred_element_type=F32)


def lane_gather(table, index):
    return jnp.take_along_axis(table, index, axis=1, mode="promise_in_bounds")


def owner_at(chunk, i):
    y, u = i // 2, i % 2
    return y * NZ + (chunk + 4 * u - 2 * y + 2 * NZ) % NZ


def twice(x):
    return jnp.transpose(jnp.concatenate([x, pltpu.roll(x, 96, axis=1)], axis=0))


def columns(x):
    return jnp.transpose(jnp.concatenate([x] * 16, axis=0))


def kernel(
    n, lab_ref, q_ref, id_ref, mask_ref, mlab_ref, mem_hbm, prec_ref, grad_ref,
    mem_ref, tab_ref, qall, tall, idall, s_ref, st_ref, inv_ref, ct_ref,
    ppart, prs, pown, pall, pt_ref, wq_ref, aux_ref,
    rsum, rpart, rrs, wdown, wdall, wt_ref, gpart, grs,
    send_sem, recv_sem, mem_sem,
):
    me = lax.axis_index("shard")
    rows = mem_ref.shape[0]
    base = me * rows
    nb = rows // 128
    my_y, my_z = me // NZ, me % NZ
    turn = my_z + 2 * my_y
    my_chunk = turn % NC
    my_place = my_chunk * NO + 2 * my_y + (turn % NZ) // NC

    def along_z(d):
        return my_y * NZ + (my_z + d) % NZ

    def along_y(d):
        return ((my_y + d) % NY) * NZ + my_z

    barrier = pltpu.get_barrier_semaphore()
    for peer in [along_z(d) for d in range(1, NZ)] + [along_y(d) for d in range(1, NY)]:
        pl.semaphore_signal(barrier, inc=1, device_id={"shard": peer}, device_id_type=MESH)

    load_memory = pltpu.make_async_copy(mem_hbm, mem_ref, mem_sem)
    load_memory.start()

    row = lax.broadcasted_iota(I32, (8, 64), 0)
    label = jnp.zeros((8, 64), I32)
    for i in range(8):
        label = jnp.where(row == i, lab_ref[i], label)
    tab_ref[:, 0:64] = jnp.where(mask_ref[...] > 0, id_ref[...], -1)
    tab_ref[:, 64:128] = label
    qall[me] = q_ref[...]
    tall[me] = tab_ref[...]

    def put(src, dst, send, recv, peer):
        pltpu.make_async_remote_copy(
            src_ref=src, dst_ref=dst, send_sem=send_sem.at[send], recv_sem=recv_sem.at[recv],
            device_id={"shard": peer}, device_id_type=MESH,
        ).start()

    def await_blocks(sem, index, buf, count):
        view = buf.at[pl.ds(0, count)]
        pltpu.make_async_copy(view, view, sem.at[index]).wait()

    pl.semaphore_wait(barrier, NZ + NY - 2)
    for d in (4, 3, 5, 2, 6, 1, 7):
        put(q_ref, qall.at[me], 0, 0, along_z(d))
        put(tab_ref, tall.at[me], 1, 1, along_z(d))
    line = pl.ds(my_y * NZ, NZ)
    await_blocks(recv_sem, 0, qall, NZ - 1)
    for d in (2, 1, 3):
        put(qall.at[line], qall.at[line], 0, 2, along_y(d))
    await_blocks(recv_sem, 1, tall, NZ - 1)
    for d in (2, 1, 3):
        put(tall.at[line], tall.at[line], 1, 3, along_y(d))
    load_memory.wait()
    await_blocks(recv_sem, 2, qall, n - NZ)
    await_blocks(recv_sem, 3, tall, n - NZ)

    lane = lax.broadcasted_iota(I32, (8, 128), 1)
    width = q_ref.shape[1]

    def queries_of(c):
        return jnp.concatenate([qall[owner_at(c, i)].astype(F32) for i in range(NO)], axis=0)

    def to_owners(c, src, dst, send, recv):
        def one(j, carry):
            i = (j + me) % NO
            owner = owner_at(c, i)

            @pl.when(owner != me)
            def _():
                put(src.at[c * NO + i], dst.at[me], send, recv + c, owner)

            return carry

        lax.fori_loop(0, NO, one, 0)

    def to_all(src, dst, send, recv):
        def one(d, carry):
            put(src, dst.at[my_place], send, recv + my_chunk, (me + d) % n)
            return carry

        lax.fori_loop(1, n, one, 0)

    def await_chunk(c, recv, buf):
        @pl.when(my_chunk == c)
        def _():
            await_blocks(recv_sem, recv + c, buf, NO - 1)

        @pl.when(my_chunk != c)
        def _():
            await_blocks(recv_sem, recv + c, buf, NO)

    for c in range(NC):
        s_ref[...] = dot_nt(queries_of(c).astype(BF16), mem_ref[...])
        for i in range(NO):
            table = tall[owner_at(c, i)]
            idall[c * NO + i] = table
            local = table - base
            place = jnp.bitwise_and(local, 127)
            which = jnp.right_shift(local, 7)
            value = jnp.zeros((8, 128), F32)
            for a in range(nb):
                block = s_ref[i * 8 : i * 8 + 8, a * 128 : a * 128 + 128]
                value = jnp.where(which == a, lane_gather(block, place), value)
            ppart[c * NO + i] = jnp.where(lane < 64, value * HALF_INV_TAU, 0.0)
        to_owners(c, ppart, prs, 2, 4)
    prs[me] = ppart[my_place]

    mlab_t = columns(mlab_ref[...])
    for c in range(NC):
        q = queries_of(c).astype(BF16)
        q = jnp.concatenate([q, q], axis=0)
        ids = idall[c * NO : c * NO + NO].reshape(NO * 8, 128)
        labels = jnp.transpose(jnp.concatenate([ids, ids], axis=0))[64:65, :]
        for a in range(nb):
            st = dot_nt(mem_ref[a * 128 : a * 128 + 128, :], q) * HALF_INV_TAU
            column = jnp.broadcast_to(mlab_t[:, a : a + 1], (128, 128))
            st_ref[c, a * 128 : a * 128 + 128, :] = jnp.where(column != labels, st, FAR)

    def invert(b, c):
        local = idall[b] - base
        found = [jnp.full((8, 128), -1, I32) for _ in range(nb)]
        for k in range(64):
            here = jnp.broadcast_to(local[:, k : k + 1], (8, 128))
            for a in range(nb):
                found[a] = jnp.where(here == lane + a * 128, 64 + k, found[a])
        for a in range(nb):
            inv_ref[b, :, a * 128 : a * 128 + 128] = found[a]
        return c

    lax.fori_loop(0, SPLIT, invert, 0)

    await_blocks(recv_sem, 4 + my_chunk, prs, n - 1)
    own = jnp.sum(prs[...], axis=0)
    pown[...] = own
    to_all(pown, pall, 3, 8)
    pall[my_place] = own

    mask = jnp.where(jnp.logical_and(lane < 64, tab_ref[...] >= 0), 1.0, 0.0)
    own_t = columns(own)
    mask_t = columns(mask)
    off = jnp.where(
        lax.broadcasted_iota(I32, (64, 128), 0) == lax.broadcasted_iota(I32, (64, 128), 1), 0.0, 1.0
    )
    for i in range(8):
        col = jnp.broadcast_to(own_t[:64, i : i + 1], (64, 128))
        mcol = jnp.broadcast_to(mask_t[:64, i : i + 1], (64, 128)) * off
        t = jnp.tanh(col - own[i : i + 1, :])
        w = (1.0 - t * t) * (0.25 * off)
        wq_ref[i] = w
        aux_ref[i : i + 1, :] = 1.0 + jnp.sum(mcol * (0.5 + 0.5 * t), axis=0, keepdims=True)
        aux_ref[8 + i : 9 + i, :] = jnp.sum(mcol * w, axis=0, keepdims=True)
    rsum[...] = jnp.zeros_like(rsum)

    lax.fori_loop(SPLIT, n, invert, 0)

    def first_pass(c, carry):
        await_chunk(c, 8, pall)
        pt_ref[c] = twice(pall[pl.ds(c * NO, NO)].reshape(NO * 8, 128))[:32, :]

        def slots(kb, carry):
            p = [
                jnp.broadcast_to(pt_ref[c, pl.ds(kb * KB + i, 1), :], (8, 128)) for i in range(KB)
            ]

            def step(g, acc):
                acc = list(acc)
                s = [
                    st_ref[c, pl.ds(pl.multiple_of(g * (8 * G), 8 * G) + 8 * v, 8), :]
                    for v in range(G)
                ]
                for i in range(KB):
                    one = two = None
                    for v in range(G):
                        t = jnp.tanh(s[v] - p[i])
                        one = t if one is None else one + t
                        two = t * t if two is None else two + t * t
                    acc[2 * i] = acc[2 * i] + (one + float(G))
                    acc[2 * i + 1] = acc[2 * i + 1] + (float(G) - two)
                return tuple(acc)

            zero = jnp.zeros((8, 128), F32)
            acc = lax.fori_loop(0, rows // (8 * G), step, (zero,) * (2 * KB), unroll=4)
            for i in range(KB):
                rsum[pl.ds(kb * KB + i, 1), :] = 0.5 * jnp.sum(acc[2 * i], axis=0, keepdims=True)
                rsum[pl.ds(64 + kb * KB + i, 1), :] = 0.25 * jnp.sum(
                    acc[2 * i + 1], axis=0, keepdims=True
                )
            return carry

        lax.fori_loop(0, 32 // KB, slots, 0)
        both = jnp.transpose(rsum[...])
        both = both[:64, :] + pltpu.roll(both[64:, :], 32, axis=1)
        rpart[pl.ds(c * NO, NO)] = both.reshape(NO, 8, 128)
        to_owners(c, rpart, rrs, 4, 12)
        return carry

    lax.fori_loop(0, NC, first_pass, 0)

    rrs[me] = rpart[my_place]
    await_blocks(recv_sem, 12 + my_chunk, rrs, n - 1)
    rank_neg = jnp.sum(rrs[...], axis=0)
    slope_neg = pltpu.roll(rank_neg, 64, axis=1)
    rank_pos = aux_ref[0:8, :]
    spread = aux_ref[8:16, :]
    total = rank_pos + rank_neg
    found = jnp.sum(mask, axis=1, keepdims=True)
    share = mask / (found * total * total)
    weight_neg = share * rank_pos
    weight_pos = -share * rank_neg
    wp_t = columns(weight_pos)
    for i in range(8):
        col = jnp.broadcast_to(wp_t[:64, i : i + 1], (64, 128))
        aux_ref[16 + i : 17 + i, :] = jnp.sum(col * wq_ref[i], axis=0, keepdims=True)
    backed = aux_ref[16:24, :]
    dpos = (mask * backed - weight_neg * slope_neg - weight_pos * spread) * (2.0 * HALF_INV_TAU)
    both = jnp.where(lane < 64, weight_neg * (0.5 * HALF_INV_TAU), pltpu.roll(dpos, 64, axis=1))
    wdown[...] = both
    to_all(wdown, wdall, 5, 16)
    wdall[my_place] = both
    precision = jnp.sum(mask * rank_pos / total, axis=1, keepdims=True) / found
    for i in range(8):
        prec_ref[i] = precision[i, 0]

    def second_pass(c, carry):
        await_chunk(c, 16, wdall)
        wt_ref[...] = twice(wdall[pl.ds(c * NO, NO)].reshape(NO * 8, 128))[:32, :]

        def block(jb, carry):
            start = pl.multiple_of(jb * (8 * JB), 8 * JB)
            s = [st_ref[c, pl.ds(start + 8 * v, 8), :] for v in range(JB)]

            def slot(k, acc):
                p = jnp.broadcast_to(pt_ref[c, pl.ds(k, 1), :], (8, 128))
                w = jnp.broadcast_to(wt_ref[pl.ds(k, 1), :], (8, 128))
                out = []
                for v in range(JB):
                    t = jnp.tanh(s[v] - p)
                    out.append(acc[v] + w * (1.0 - t * t))
                return tuple(out)

            zero = jnp.zeros((8, 128), F32)
            acc = lax.fori_loop(0, 32, slot, (zero,) * JB, unroll=16)
            for v in range(JB):
                ct_ref[pl.ds(start + 8 * v, 8), :] = acc[v]
            return carry

        lax.fori_loop(0, rows // (8 * JB), block, 0)
        hi, lo = [], []
        for a in range(nb):
            neg = jnp.transpose(ct_ref[a * 128 : a * 128 + 128, :])
            pos = []
            for i in range(NO):
                index = inv_ref[c * NO + i, :, a * 128 : a * 128 + 128]
                value = lane_gather(wdall[c * NO + i], jnp.bitwise_and(index, 127))
                pos.append(jnp.where(index >= 0, value, 0.0))
            cot = neg[:64, :] + neg[64:, :] + jnp.concatenate(pos, axis=0)
            top = cot.astype(BF16).astype(F32)
            hi.append(top)
            lo.append(cot - top)
        cot = jnp.concatenate([jnp.concatenate(hi, axis=1), jnp.concatenate(lo, axis=1)], axis=0)
        grad = dot_nn(cot.astype(BF16), mem_ref[...])
        gpart[pl.ds(c * NO, NO)] = (grad[:64, :] + grad[64:, :]).reshape(NO, 8, width)
        to_owners(c, gpart, grs, 6, 20)
        return carry

    lax.fori_loop(0, NC, second_pass, 0)

    grs[me] = gpart[my_place]
    await_blocks(recv_sem, 20 + my_chunk, grs, n - 1)
    grad_ref[...] = jnp.sum(grs[...], axis=0)
    for send, buf in enumerate((qall, tall, ppart, pall, rpart, wdall, gpart)):
        await_blocks(send_sem, send, buf, n - 1)


def on_device(n, queries, query_labels, positive_ids, positive_mask, memory, memory_labels):
    own, width = queries.shape
    rows = memory.shape[0]
    vmem = pl.BlockSpec(memory_space=pltpu.VMEM)
    smem = pl.BlockSpec(memory_space=pltpu.SMEM)
    return pl.pallas_call(
        functools.partial(kernel, n),
        out_shape=(
            jax.ShapeDtypeStruct((own,), F32),
            jax.ShapeDtypeStruct((own, width), F32),
        ),
        in_specs=[smem, vmem, vmem, vmem, vmem, pl.BlockSpec(memory_space=pl.ANY)],
        out_specs=(smem, vmem),
        scratch_shapes=[
            pltpu.VMEM((rows, width), BF16),
            pltpu.VMEM((own, 128), I32),
            pltpu.VMEM((n, own, width), BF16),
            pltpu.VMEM((n, own, 128), I32),
            pltpu.VMEM((n, own, 128), I32),
            pltpu.VMEM((NO * own, rows), F32),
            pltpu.VMEM((NC, rows, 128), F32),
            pltpu.VMEM((n, own, rows), I32),
            pltpu.VMEM((rows, 128), F32),
            pltpu.VMEM((n, own, 128), F32),
            pltpu.VMEM((n, own, 128), F32),
            pltpu.VMEM((own, 128), F32),
            pltpu.VMEM((n, own, 128), F32),
            pltpu.VMEM((NC, 32, 128), F32),
            pltpu.VMEM((own, 64, 128), F32),
            pltpu.VMEM((24, 128), F32),
            pltpu.VMEM((128, 128), F32),
            pltpu.VMEM((n, own, 128), F32),
            pltpu.VMEM((n, own, 128), F32),
            pltpu.VMEM((own, 128), F32),
            pltpu.VMEM((n, own, 128), F32),
            pltpu.VMEM((32, 128), F32),
            pltpu.VMEM((n, own, width), F32),
            pltpu.VMEM((n, own, width), F32),
            pltpu.SemaphoreType.DMA((7,)),
            pltpu.SemaphoreType.DMA((24,)),
            pltpu.SemaphoreType.DMA,
        ],
        compiler_params=pltpu.CompilerParams(collective_id=0, has_side_effects=True),
    )(
        query_labels, queries, positive_ids, positive_mask,
        memory_labels.reshape(rows // 128, 128), memory,
    )


def solution(mesh):
    n = mesh.shape["shard"]
    return jax.shard_map(
        functools.partial(on_device, n),
        mesh=mesh,
        in_specs=(
            P(("dp", "shard"), None),
            P(("dp", "shard")),
            P(("dp", "shard"), None),
            P(("dp", "shard"), None),
            P("shard", None),
            P("shard"),
        ),
        out_specs=(P(("dp", "shard")), P(("dp", "shard"), None)),
        check_vma=False,
    )
```

```python
import functools

import jax
import jax.numpy as jnp
from jax import lax
from jax.experimental import pallas as pl
from jax.experimental.pallas import tpu as pltpu
from jax.sharding import PartitionSpec as P

F32 = jnp.float32
BF16 = jnp.bfloat16
I32 = jnp.int32
HALF_INV_TAU = 5.0
FAR = -1e6
MESH = pl.DeviceIdType.MESH
G = 16
KB = 8
JB = 8
JC = 16
NY, NZ = 4, 8
NC, NO = 4, 8
Z_IN, Z_TAB, Y_IN, Y_TAB, POS, POS_ALL, RANK, WEIGHT, GRAD, SPARE, N_RECV = (
    0, 8, 16, 17, 18, 22, 26, 30, 34, 38, 41,
)
VMEM_LIMIT = 60 * 1024 * 1024
SPLIT = 12


def dot_nt(a, b):
    return lax.dot_general(a, b, (((1,), (1,)), ((), ())), preferred_element_type=F32)


def dot_nn(a, b):
    return lax.dot_general(a, b, (((1,), (0,)), ((), ())), preferred_element_type=F32)


def lane_gather(table, index):
    return jnp.take_along_axis(table, index, axis=1, mode="promise_in_bounds")


def static_owner_at(chunk, i):
    y, u = i // 2, i % 2
    return y * NZ + (chunk + 4 * u - 2 * y + 2 * NZ) % NZ


def owner_at(chunk, i):
    y, u = i // 2, i % 2
    return y * NZ + lax.rem(chunk + (4 * u - 2 * y + 2 * NZ), NZ)


def twice(x):
    return jnp.transpose(jnp.concatenate([x, pltpu.roll(x, 96, axis=1)], axis=0))


def columns(x):
    return jnp.transpose(jnp.concatenate([x] * 16, axis=0))


def kernel(
    n, lab_ref, q_ref, id_ref, mask_ref, mlab_ref, mem_hbm, prec_ref, grad_ref,
    mem_ref, tab_ref, qall, tall, idall, s_ref, st_ref, inv_ref, ct_ref,
    ppart, prs, pown, pall, pt_ref, wq_ref, aux_ref,
    racc, squares, rpart, rrs, wdown, wdall, wt_ref, gpart, grs,
    send_sem, recv_sem, mem_sem,
):
    me = lax.axis_index("shard")
    rows = mem_ref.shape[0]
    base = me * rows
    nb = rows // 128
    my_y, my_z = lax.div(me, NZ), lax.rem(me, NZ)
    turn = lax.rem(my_z + 2 * my_y, NZ)
    my_chunk = lax.rem(turn, NC)
    my_place = my_chunk * NO + 2 * my_y + lax.div(turn, NC)
    y_of = [lax.rem(my_y + d, NY) * NZ for d in range(NY)]
    z_of = [lax.rem(my_z + d, NZ) for d in range(NZ)]

    def along_z(d):
        return y_of[0] + z_of[d]

    def along_y(d):
        return y_of[d] + z_of[0]

    barrier = pltpu.get_barrier_semaphore()
    for peer in [along_z(d) for d in range(1, NZ)] + [along_y(d) for d in range(1, NY)]:
        pl.semaphore_signal(barrier, inc=1, device_id={"shard": peer}, device_id_type=MESH)

    load_memory = pltpu.make_async_copy(mem_hbm, mem_ref, mem_sem)
    load_memory.start()

    row = lax.broadcasted_iota(I32, (8, 64), 0)
    label = jnp.zeros((8, 64), I32)
    for i in range(8):
        label = jnp.where(row == i, lab_ref[i], label)
    tab_ref[:, 0:64] = jnp.where(mask_ref[...] > 0, id_ref[...], -1)
    tab_ref[:, 64:128] = label
    qall[me] = q_ref[...]
    tall[me] = tab_ref[...]

    def put(src, dst, send, recv, peer):
        pltpu.make_async_remote_copy(
            src_ref=src, dst_ref=dst, send_sem=send_sem.at[send], recv_sem=recv_sem.at[recv],
            device_id={"shard": peer}, device_id_type=MESH,
        ).start()

    def await_blocks(sem, index, buf, count):
        view = buf.at[pl.ds(0, count)]
        pltpu.make_async_copy(view, view, sem.at[index]).wait()

    pl.semaphore_wait(barrier, NZ + NY - 2)
    for d in (4, 3, 5, 2, 6, 1, 7):
        put(q_ref, qall.at[me], 0, Z_IN + my_z, along_z(d))
        put(tab_ref, tall.at[me], 1, Z_TAB + my_z, along_z(d))
    for d in (2, 1, 3):
        put(q_ref, qall.at[me], 0, Y_IN, along_y(d))
        put(tab_ref, tall.at[me], 1, Y_TAB, along_y(d))
    for d in (1, 7, 2, 6, 3, 5, 4):
        slot = along_z(d)
        pltpu.make_async_copy(qall.at[slot], qall.at[slot], recv_sem.at[Z_IN + z_of[d]]).wait()
        for dy in (2, 1, 3):
            put(qall.at[slot], qall.at[slot], 0, Y_IN, along_y(dy))
        pltpu.make_async_copy(tall.at[slot], tall.at[slot], recv_sem.at[Z_TAB + z_of[d]]).wait()
        for dy in (2, 1, 3):
            put(tall.at[slot], tall.at[slot], 1, Y_TAB, along_y(dy))
    load_memory.wait()
    await_blocks(recv_sem, Y_IN, qall, n - NZ)
    await_blocks(recv_sem, Y_TAB, tall, n - NZ)

    lane = lax.broadcasted_iota(I32, (8, 128), 1)
    width = q_ref.shape[1]

    def queries_of(c):
        return jnp.concatenate([qall[static_owner_at(c, i)].astype(F32) for i in range(NO)], axis=0)

    def to_owners(c, src, dst, send, recv, spare):
        for i in range(NO):
            owner = owner_at(c, i)
            mine = owner == me
            put(
                src.at[c * NO + i], dst.at[jnp.where(mine, n, me)], send,
                jnp.where(mine, spare, recv + c), jnp.where(mine, along_z(1), owner),
            )

    def to_all(src, dst, send, recv):
        offsets = [(dy, dz) for dy in range(NY) for dz in range(NZ) if dy or dz]
        offsets.sort(key=lambda o: -min(o[0], NY - o[0]) - min(o[1], NZ - o[1]))
        for dy, dz in offsets:
            put(src, dst.at[my_place], send, recv + my_chunk, y_of[dy] + z_of[dz])

    def await_chunk(c, recv, buf):
        @pl.when(my_chunk == c)
        def _():
            await_blocks(recv_sem, recv + c, buf, NO - 1)

        @pl.when(my_chunk != c)
        def _():
            await_blocks(recv_sem, recv + c, buf, NO)

    for c in range(NC):
        s_ref[...] = dot_nt(queries_of(c).astype(BF16), mem_ref[...])
        for i in range(NO):
            table = tall[static_owner_at(c, i)]
            idall[c * NO + i] = table
            local = table - base
            place = jnp.bitwise_and(local, 127)
            which = jnp.right_shift(local, 7)
            value = jnp.zeros((8, 128), F32)
            for a in range(nb):
                block = s_ref[i * 8 : i * 8 + 8, a * 128 : a * 128 + 128]
                value = jnp.where(which == a, lane_gather(block, place), value)
            ppart[c * NO + i] = jnp.where(lane < 64, value * HALF_INV_TAU, 0.0)
        to_owners(c, ppart, prs, 2, POS, SPARE)
    prs[me] = ppart[my_place]

    mlab_t = columns(mlab_ref[...])
    for c in range(NC):
        q = queries_of(c).astype(BF16)
        q = jnp.concatenate([q, q], axis=0)
        ids = idall[c * NO : c * NO + NO].reshape(NO * 8, 128)
        labels = jnp.transpose(jnp.concatenate([ids, ids], axis=0))[64:65, :]
        for a in range(nb):
            st = dot_nt(mem_ref[a * 128 : a * 128 + 128, :], q) * HALF_INV_TAU
            column = jnp.broadcast_to(mlab_t[:, a : a + 1], (128, 128))
            st_ref[c, a * 128 : a * 128 + 128, :] = jnp.where(column != labels, st, FAR)

    def invert(b, c):
        local = idall[b] - base
        found = [jnp.full((8, 128), -1, I32) for _ in range(nb)]
        for k in range(64):
            here = jnp.broadcast_to(local[:, k : k + 1], (8, 128))
            for a in range(nb):
                found[a] = jnp.where(here == lane + a * 128, 64 + k, found[a])
        for a in range(nb):
            inv_ref[b, :, a * 128 : a * 128 + 128] = found[a]
        return c

    lax.fori_loop(0, SPLIT, invert, 0)

    await_blocks(recv_sem, POS + my_chunk, prs, n - 1)
    own = jnp.sum(prs[0:n], axis=0)
    pown[...] = own
    to_all(pown, pall, 3, POS_ALL)
    pall[my_place] = own

    mask = jnp.where(jnp.logical_and(lane < 64, tab_ref[...] >= 0), 1.0, 0.0)
    own_t = columns(own)
    mask_t = columns(mask)
    off = jnp.where(
        lax.broadcasted_iota(I32, (64, 128), 0) == lax.broadcasted_iota(I32, (64, 128), 1), 0.0, 1.0
    )
    for i in range(8):
        col = jnp.broadcast_to(own_t[:64, i : i + 1], (64, 128))
        mcol = jnp.broadcast_to(mask_t[:64, i : i + 1], (64, 128)) * off
        t = jnp.tanh(col - own[i : i + 1, :])
        w = (1.0 - t * t) * (0.25 * off)
        wq_ref[i] = w
        aux_ref[i : i + 1, :] = 1.0 + jnp.sum(mcol * (0.5 + 0.5 * t), axis=0, keepdims=True)
        aux_ref[8 + i : 9 + i, :] = jnp.sum(mcol * w, axis=0, keepdims=True)

    lax.fori_loop(SPLIT, n, invert, 0)

    zero = jnp.zeros((8, 128), F32)

    def first_pass(c, keep):
        await_chunk(c, POS_ALL, pall)
        pt_ref[c] = twice(pall[pl.ds(c * NO, NO)].reshape(NO * 8, 128))[:32, :]

        def slots(kb, carry):
            p = [
                jnp.broadcast_to(pt_ref[c, pl.ds(kb * KB + i, 1), :], (8, 128)) for i in range(KB)
            ]

            def step(g, acc):
                acc = list(acc)
                at = [pl.ds(pl.multiple_of(g * (8 * G), 8 * G) + 8 * v, 8) for v in range(G)]
                for i in range(KB):
                    one = two = None
                    for v in range(G):
                        t = jnp.tanh(st_ref[c, at[v], :] - p[i])
                        tt = t * t
                        if keep:
                            squares[(c - 1) * 32 + kb * KB + i, at[v], :] = tt
                        one = t if one is None else one + t
                        two = tt if two is None else two + tt
                    acc[2 * i] = acc[2 * i] + (one + float(G))
                    acc[2 * i + 1] = acc[2 * i + 1] + (float(G) - two)
                return tuple(acc)

            acc = lax.fori_loop(0, rows // (8 * G), step, (zero,) * (2 * KB), unroll=4)
            for i in range(KB):
                racc[kb * KB + i] = acc[2 * i]
                racc[32 + kb * KB + i] = acc[2 * i + 1]
            return carry

        lax.fori_loop(0, 32 // KB, slots, 0)
        sums = jnp.sum(racc[...], axis=1)
        gap = jnp.zeros((32, 128), F32)
        both = jnp.transpose(
            jnp.concatenate([0.5 * sums[:32, :], gap, 0.25 * sums[32:, :], gap], axis=0)
        )
        both = both[:64, :] + pltpu.roll(both[64:, :], 32, axis=1)
        rpart[pl.ds(c * NO, NO)] = both.reshape(NO, 8, 128)
        to_owners(c, rpart, rrs, 4, RANK, SPARE + 1)

    def with_squares(body):
        def one(c, carry):
            body(c, True)
            return carry

        lax.fori_loop(1, NC, one, 0)

    first_pass(0, False)
    with_squares(first_pass)

    rrs[me] = rpart[my_place]
    await_blocks(recv_sem, RANK + my_chunk, rrs, n - 1)
    rank_neg = jnp.sum(rrs[0:n], axis=0)
    slope_neg = pltpu.roll(rank_neg, 64, axis=1)
    rank_pos = aux_ref[0:8, :]
    spread = aux_ref[8:16, :]
    total = rank_pos + rank_neg
    found = jnp.sum(mask, axis=1, keepdims=True)
    share = mask / (found * total * total)
    weight_neg = share * rank_pos
    weight_pos = -share * rank_neg
    wp_t = columns(weight_pos)
    for i in range(8):
        col = jnp.broadcast_to(wp_t[:64, i : i + 1], (64, 128))
        aux_ref[16 + i : 17 + i, :] = jnp.sum(col * wq_ref[i], axis=0, keepdims=True)
    backed = aux_ref[16:24, :]
    dpos = (mask * backed - weight_neg * slope_neg - weight_pos * spread) * (2.0 * HALF_INV_TAU)
    both = jnp.where(lane < 64, weight_neg * (0.5 * HALF_INV_TAU), pltpu.roll(dpos, 64, axis=1))
    wdown[...] = both
    to_all(wdown, wdall, 5, WEIGHT)
    wdall[my_place] = both
    precision = jnp.sum(mask * rank_pos / total, axis=1, keepdims=True) / found
    for i in range(8):
        prec_ref[i] = precision[i, 0]

    def second_pass(c, kept):
        await_chunk(c, WEIGHT, wdall)
        wt_ref[...] = twice(wdall[pl.ds(c * NO, NO)].reshape(NO * 8, 128))[:32, :]
        groups = JC if kept else JB

        def block(jb, carry):
            start = pl.multiple_of(jb * (8 * groups), 8 * groups)
            at = [pl.ds(start + 8 * v, 8) for v in range(groups)]
            acc = [zero] * groups
            for k in range(32):
                w = jnp.broadcast_to(wt_ref[k : k + 1, :], (8, 128))
                if not kept:
                    p = jnp.broadcast_to(pt_ref[c, k : k + 1, :], (8, 128))
                for v in range(groups):
                    if kept:
                        tt = squares[(c - 1) * 32 + k, at[v], :]
                    else:
                        t = jnp.tanh(st_ref[c, at[v], :] - p)
                        tt = t * t
                    acc[v] = acc[v] + w * (1.0 - tt)
            for v in range(groups):
                ct_ref[at[v], :] = acc[v]
            return carry

        lax.fori_loop(0, rows // (8 * groups), block, 0)
        hi, lo = [], []
        for a in range(nb):
            neg = jnp.transpose(ct_ref[a * 128 : a * 128 + 128, :])
            pos = []
            for i in range(NO):
                index = inv_ref[c * NO + i, :, a * 128 : a * 128 + 128]
                value = lane_gather(wdall[c * NO + i], jnp.bitwise_and(index, 127))
                pos.append(jnp.where(index >= 0, value, 0.0))
            cot = neg[:64, :] + neg[64:, :] + jnp.concatenate(pos, axis=0)
            top = cot.astype(BF16).astype(F32)
            hi.append(top)
            lo.append(cot - top)
        cot = jnp.concatenate([jnp.concatenate(hi, axis=1), jnp.concatenate(lo, axis=1)], axis=0)
        grad = dot_nn(cot.astype(BF16), mem_ref[...])
        gpart[pl.ds(c * NO, NO)] = (grad[:64, :] + grad[64:, :]).reshape(NO, 8, width)
        to_owners(c, gpart, grs, 6, GRAD, SPARE + 2)

    second_pass(0, False)
    with_squares(second_pass)

    grs[me] = gpart[my_place]
    await_blocks(recv_sem, GRAD + my_chunk, grs, n - 1)
    grad_ref[...] = jnp.sum(grs[0:n], axis=0)
    for i, buf in enumerate((prs, rrs, grs)):
        await_blocks(recv_sem, SPARE + i, buf, 1)
    for send, buf in enumerate((qall, tall, ppart, pall, rpart, wdall, gpart)):
        await_blocks(send_sem, send, buf, n if send in (2, 4, 6) else n - 1)


def on_device(n, queries, query_labels, positive_ids, positive_mask, memory, memory_labels):
    own, width = queries.shape
    rows = memory.shape[0]
    vmem = pl.BlockSpec(memory_space=pltpu.VMEM)
    smem = pl.BlockSpec(memory_space=pltpu.SMEM)
    return pl.pallas_call(
        functools.partial(kernel, n),
        out_shape=(
            jax.ShapeDtypeStruct((own,), F32),
            jax.ShapeDtypeStruct((own, width), F32),
        ),
        in_specs=[smem, vmem, vmem, vmem, vmem, pl.BlockSpec(memory_space=pltpu.HBM)],
        out_specs=(smem, vmem),
        scratch_shapes=[
            pltpu.VMEM((rows, width), BF16),
            pltpu.VMEM((own, 128), I32),
            pltpu.VMEM((n, own, width), BF16),
            pltpu.VMEM((n, own, 128), I32),
            pltpu.VMEM((n, own, 128), I32),
            pltpu.VMEM((NO * own, rows), F32),
            pltpu.VMEM((NC, rows, 128), F32),
            pltpu.VMEM((n, own, rows), I32),
            pltpu.VMEM((rows, 128), F32),
            pltpu.VMEM((n, own, 128), F32),
            pltpu.VMEM((n + 1, own, 128), F32),
            pltpu.VMEM((own, 128), F32),
            pltpu.VMEM((n, own, 128), F32),
            pltpu.VMEM((NC, 32, 128), F32),
            pltpu.VMEM((own, 64, 128), F32),
            pltpu.VMEM((24, 128), F32),
            pltpu.VMEM((64, 8, 128), F32),
            pltpu.VMEM(((NC - 1) * 32, rows, 128), F32),
            pltpu.VMEM((n, own, 128), F32),
            pltpu.VMEM((n + 1, own, 128), F32),
            pltpu.VMEM((own, 128), F32),
            pltpu.VMEM((n, own, 128), F32),
            pltpu.VMEM((32, 128), F32),
            pltpu.VMEM((n, own, width), F32),
            pltpu.VMEM((n + 1, own, width), F32),
            pltpu.SemaphoreType.DMA((7,)),
            pltpu.SemaphoreType.DMA((N_RECV,)),
            pltpu.SemaphoreType.DMA,
        ],
        compiler_params=pltpu.CompilerParams(
            collective_id=0, has_side_effects=True, vmem_limit_bytes=VMEM_LIMIT
        ),
    )(
        query_labels, queries, positive_ids, positive_mask,
        memory_labels.reshape(rows // 128, 128), memory,
    )


def solution(mesh):
    n = mesh.shape["shard"]
    return jax.shard_map(
        functools.partial(on_device, n),
        mesh=mesh,
        in_specs=(
            P(("dp", "shard"), None),
            P(("dp", "shard")),
            P(("dp", "shard"), None),
            P(("dp", "shard"), None),
            P("shard", None),
            P("shard"),
        ),
        out_specs=(P(("dp", "shard")), P(("dp", "shard"), None)),
        check_vma=False,
    )
```

```python
import functools

import jax
import jax.numpy as jnp
from jax import lax
from jax.experimental import pallas as pl
from jax.experimental.pallas import tpu as pltpu
from jax.sharding import PartitionSpec as P

F32 = jnp.float32
BF16 = jnp.bfloat16
I32 = jnp.int32
I16 = jnp.int16
HALF_INV_TAU = 5.0
FAR = -1e6
MESH = pl.DeviceIdType.MESH
G = 32
KB = 8
JB = 8
JC = 16
NY, NZ = 4, 8
NC, NO = 4, 8
Z_IN, Z_TAB, Y_IN, Y_TAB, POS_Z, POS_Y, RANK, WEIGHT, GRAD, SPARE, N_RECV = (
    0, 8, 16, 17, 18, 22, 26, 30, 34, 38, 40,
)
VMEM_LIMIT = 60 * 1024 * 1024


def dot_nt(a, b):
    return lax.dot_general(a, b, (((1,), (1,)), ((), ())), preferred_element_type=F32)


def dot_nn(a, b):
    return lax.dot_general(a, b, (((1,), (0,)), ((), ())), preferred_element_type=F32)


def lane_gather(table, index):
    return jnp.take_along_axis(table, index, axis=1, mode="promise_in_bounds")


def static_owner_at(chunk, i):
    y, u = i // 2, i % 2
    return y * NZ + (chunk + 4 * u - 2 * y + 2 * NZ) % NZ


def owner_at(chunk, i):
    y, u = i // 2, i % 2
    return y * NZ + lax.rem(chunk + (4 * u - 2 * y + 2 * NZ), NZ)


def twice(x):
    return jnp.transpose(jnp.concatenate([x, pltpu.roll(x, 96, axis=1)], axis=0))


def columns(x):
    return jnp.transpose(jnp.concatenate([x] * 16, axis=0))


def kernel(
    n, lab_ref, q_ref, id_ref, mask_ref, mlab_ref, mem_hbm, prec_ref, grad_ref,
    mem_ref, tab_ref, half_ref, qall, tall, idall, s_ref, st_ref, inv_ref, ct_ref,
    ppart, pz, pys, py, pos_ref, pt_ref, wq_ref, aux_ref,
    racc, squares, rpart, rrs, wdown, wdall, wt_ref, gpart, grs,
    send_sem, recv_sem, mem_sem,
):
    me = lax.axis_index("shard")
    rows = mem_ref.shape[0]
    base = me * rows
    nb = rows // 128
    my_y, my_z = lax.div(me, NZ), lax.rem(me, NZ)
    turn = lax.rem(my_z + 2 * my_y, NZ)
    my_chunk = lax.rem(turn, NC)
    my_place = my_chunk * NO + 2 * my_y + lax.div(turn, NC)
    y_of = [lax.rem(my_y + d, NY) * NZ for d in range(NY)]
    z_of = [lax.rem(my_z + d, NZ) for d in range(NZ)]

    def along_z(d):
        return y_of[0] + z_of[d]

    def along_y(d):
        return y_of[d] + z_of[0]

    barrier = pltpu.get_barrier_semaphore()
    for peer in [along_z(d) for d in range(1, NZ)] + [along_y(d) for d in range(1, NY)]:
        pl.semaphore_signal(barrier, inc=1, device_id={"shard": peer}, device_id_type=MESH)

    load_memory = pltpu.make_async_copy(mem_hbm, mem_ref, mem_sem)
    load_memory.start()

    row = lax.broadcasted_iota(I32, (8, 64), 0)
    label = jnp.zeros((8, 64), I32)
    for i in range(8):
        label = jnp.where(row == i, lab_ref[i], label)
    tab_ref[:, 0:64] = jnp.where(mask_ref[...] > 0, id_ref[...], -1)
    tab_ref[:, 64:128] = label
    qall[me] = q_ref[...]
    half_ref[...] = tab_ref[...].astype(I16)
    tall[me] = half_ref[...]

    def put(src, dst, send, recv, peer):
        pltpu.make_async_remote_copy(
            src_ref=src, dst_ref=dst, send_sem=send_sem.at[send], recv_sem=recv_sem.at[recv],
            device_id={"shard": peer}, device_id_type=MESH,
        ).start()

    def await_blocks(sem, index, buf, count):
        view = buf.at[pl.ds(0, count)]
        pltpu.make_async_copy(view, view, sem.at[index]).wait()

    pl.semaphore_wait(barrier, NZ + NY - 2)
    for d in (4, 3, 5, 2, 6, 1, 7):
        put(q_ref, qall.at[me], 0, Z_IN + my_z, along_z(d))
        put(half_ref, tall.at[me], 1, Z_TAB + my_z, along_z(d))
    for d in (2, 1, 3):
        put(q_ref, qall.at[me], 0, Y_IN, along_y(d))
        put(half_ref, tall.at[me], 1, Y_TAB, along_y(d))
    for d in (1, 7, 2, 6, 3, 5, 4):
        slot = along_z(d)
        pltpu.make_async_copy(qall.at[slot], qall.at[slot], recv_sem.at[Z_IN + z_of[d]]).wait()
        for dy in (2, 1, 3):
            put(qall.at[slot], qall.at[slot], 0, Y_IN, along_y(dy))
        pltpu.make_async_copy(tall.at[slot], tall.at[slot], recv_sem.at[Z_TAB + z_of[d]]).wait()
        for dy in (2, 1, 3):
            put(tall.at[slot], tall.at[slot], 1, Y_TAB, along_y(dy))
    load_memory.wait()
    await_blocks(recv_sem, Y_IN, qall, n - NZ)
    await_blocks(recv_sem, Y_TAB, tall, n - NZ)

    lane = lax.broadcasted_iota(I32, (8, 128), 1)
    width = q_ref.shape[1]

    def queries_of(c):
        return jnp.concatenate([qall[static_owner_at(c, i)].astype(F32) for i in range(NO)], axis=0)

    def to_owners(c, src, dst, send, recv, spare):
        for i in range(NO):
            owner = owner_at(c, i)
            mine = owner == me
            put(
                src.at[c * NO + i], dst.at[jnp.where(mine, n, me)], send,
                jnp.where(mine, spare, recv + c), jnp.where(mine, along_z(1), owner),
            )

    def to_all(src, dst, send, recv):
        offsets = [(dy, dz) for dy in range(NY) for dz in range(NZ) if dy or dz]
        offsets.sort(key=lambda o: -min(o[0], NY - o[0]) - min(o[1], NZ - o[1]))
        for dy, dz in offsets:
            put(src, dst.at[my_place], send, recv + my_chunk, y_of[dy] + z_of[dz])

    def await_chunk(c, recv, buf):
        @pl.when(my_chunk == c)
        def _():
            await_blocks(recv_sem, recv + c, buf, NO - 1)

        @pl.when(my_chunk != c)
        def _():
            await_blocks(recv_sem, recv + c, buf, NO)

    mlab_t = columns(mlab_ref[...])

    def invert(b, c):
        local = idall[b] - base
        found = [jnp.full((8, 128), -1, I32) for _ in range(nb)]
        for k in range(64):
            here = jnp.broadcast_to(local[:, k : k + 1], (8, 128))
            for a in range(nb):
                found[a] = jnp.where(here == lane + a * 128, 64 + k, found[a])
        for a in range(nb):
            inv_ref[b, :, a * 128 : a * 128 + 128] = found[a]
        return c

    for c in range(NC):
        q = queries_of(c).astype(BF16)
        s_ref[...] = dot_nt(q, mem_ref[...])
        for i in range(NO):
            table = tall[static_owner_at(c, i)].astype(I32)
            idall[c * NO + i] = table
            local = table - base
            place = jnp.bitwise_and(local, 127)
            which = jnp.right_shift(local, 7)
            value = jnp.zeros((8, 128), F32)
            for a in range(nb):
                block = s_ref[i * 8 : i * 8 + 8, a * 128 : a * 128 + 128]
                value = jnp.where(which == a, lane_gather(block, place), value)
            value = jnp.where(lane < 64, value * HALF_INV_TAU, 0.0)
            if i < NO // 2:
                ppart[c, i] = value
            else:
                ppart[c, i - NO // 2] = ppart[c, i - NO // 2] + pltpu.roll(value, 64, axis=1)
        for d in (4, 3, 5, 2, 6, 1, 7):
            put(ppart.at[c], pz.at[c, my_z], 2, POS_Z + c, along_z(d))
        pz[c, my_z] = ppart[c]

        q = jnp.concatenate([q, q], axis=0)
        ids = idall[c * NO : c * NO + NO].reshape(NO * 8, 128)
        labels = jnp.transpose(jnp.concatenate([ids, ids], axis=0))[64:65, :]
        for a in range(nb):
            st = dot_nt(mem_ref[a * 128 : a * 128 + 128, :], q) * HALF_INV_TAU
            column = jnp.broadcast_to(mlab_t[:, a : a + 1], (128, 128))
            st_ref[c, a * 128 : a * 128 + 128, :] = jnp.where(column != labels, st, FAR)
        lax.fori_loop(c * NO, c * NO + NO, invert, 0)

    def positives_on(c):
        await_blocks(recv_sem, POS_Z + c, pz.at[c], NZ - 1)
        total = jnp.sum(pz[c], axis=0)
        pys[c] = total
        for d in (2, 1, 3):
            put(pys.at[c], py.at[c, my_y], 3, POS_Y + c, along_y(d))
        py[c, my_y] = total

    positives_on(0)
    positives_on(1)

    def owner_terms():
        my_i = my_place - my_chunk * NO
        block = pos_ref[my_chunk, lax.rem(my_i, NO // 2)]
        own = jnp.where(my_i >= NO // 2, pltpu.roll(block, 64, axis=1), block)
        own = jnp.where(lane < 64, own, 0.0)
        mask = jnp.where(jnp.logical_and(lane < 64, tab_ref[...] >= 0), 1.0, 0.0)
        own_t = columns(own)
        mask_t = columns(mask)
        off = jnp.where(
            lax.broadcasted_iota(I32, (64, 128), 0) == lax.broadcasted_iota(I32, (64, 128), 1), 0.0, 1.0
        )
        for i in range(8):
            col = jnp.broadcast_to(own_t[:64, i : i + 1], (64, 128))
            mcol = jnp.broadcast_to(mask_t[:64, i : i + 1], (64, 128)) * off
            t = jnp.tanh(col - own[i : i + 1, :])
            w = (1.0 - t * t) * (0.25 * off)
            wq_ref[i] = w
            aux_ref[i : i + 1, :] = 1.0 + jnp.sum(mcol * (0.5 + 0.5 * t), axis=0, keepdims=True)
            aux_ref[8 + i : 9 + i, :] = jnp.sum(mcol * w, axis=0, keepdims=True)

        rrs[me] = rpart[my_place]
        await_blocks(recv_sem, RANK + my_chunk, rrs, n - 1)
        rank_neg = jnp.sum(rrs[0:n], axis=0)
        slope_neg = pltpu.roll(rank_neg, 64, axis=1)
        rank_pos = aux_ref[0:8, :]
        spread = aux_ref[8:16, :]
        total = rank_pos + rank_neg
        found = jnp.sum(mask, axis=1, keepdims=True)
        share = mask / (found * total * total)
        weight_neg = share * rank_pos
        weight_pos = -share * rank_neg
        wp_t = columns(weight_pos)
        for i in range(8):
            col = jnp.broadcast_to(wp_t[:64, i : i + 1], (64, 128))
            aux_ref[16 + i : 17 + i, :] = jnp.sum(col * wq_ref[i], axis=0, keepdims=True)
        backed = aux_ref[16:24, :]
        dpos = (mask * backed - weight_neg * slope_neg - weight_pos * spread) * (2.0 * HALF_INV_TAU)
        both = jnp.where(lane < 64, weight_neg * (0.5 * HALF_INV_TAU), pltpu.roll(dpos, 64, axis=1))
        wdown[...] = both
        to_all(wdown, wdall, 5, WEIGHT)
        wdall[my_place] = both
        precision = jnp.sum(mask * rank_pos / total, axis=1, keepdims=True) / found
        for i in range(8):
            prec_ref[i] = precision[i, 0]

    zero = jnp.zeros((8, 128), F32)

    def first_pass(c, keep):
        await_blocks(recv_sem, POS_Y + c, py.at[c], NY - 1)
        both = jnp.sum(py[c], axis=0)
        pos_ref[c] = both
        both = both.reshape(NO * 4, 128)
        pt_ref[c] = twice(jnp.concatenate([both, pltpu.roll(both, 64, axis=1)], axis=0))[:32, :]

        def slots(kb, carry):
            p = [
                jnp.broadcast_to(pt_ref[c, pl.ds(kb * KB + i, 1), :], (8, 128)) for i in range(KB)
            ]

            def step(g, acc):
                acc = list(acc)
                at = [pl.ds(pl.multiple_of(g * (8 * G), 8 * G) + 8 * v, 8) for v in range(G)]
                for i in range(KB):
                    one = two = None
                    for v in range(G):
                        t = jnp.tanh(st_ref[c, at[v], :] - p[i])
                        tt = t * t
                        if keep:
                            squares[(c - 1) * 32 + kb * KB + i, at[v], :] = tt
                        one = t if one is None else one + t
                        two = tt if two is None else two + tt
                    acc[2 * i] = acc[2 * i] + (one + float(G))
                    acc[2 * i + 1] = acc[2 * i + 1] + (float(G) - two)
                return tuple(acc)

            acc = lax.fori_loop(0, rows // (8 * G), step, (zero,) * (2 * KB), unroll=2)
            for i in range(KB):
                racc[kb * KB + i] = acc[2 * i]
                racc[32 + kb * KB + i] = acc[2 * i + 1]
            return carry

        if keep:
            lax.fori_loop(0, 16 // KB, slots, 0)

            @pl.when(jnp.logical_and(c == NC - 1, my_chunk == 0))
            def _():
                owner_terms()

            lax.fori_loop(16 // KB, 32 // KB, slots, 0)
        else:
            lax.fori_loop(0, 32 // KB, slots, 0)
        sums = jnp.sum(racc[...], axis=1)
        gap = jnp.zeros((32, 128), F32)
        both = jnp.transpose(
            jnp.concatenate([0.5 * sums[:32, :], gap, 0.25 * sums[32:, :], gap], axis=0)
        )
        both = both[:64, :] + pltpu.roll(both[64:, :], 32, axis=1)
        rpart[pl.ds(c * NO, NO)] = both.reshape(NO, 8, 128)
        to_owners(c, rpart, rrs, 4, RANK, SPARE)

    def with_squares(body):
        def one(c, carry):
            body(c, True)
            return carry

        lax.fori_loop(1, NC, one, 0)

    def first_passes(c, keep):
        first_pass(c, keep)

        @pl.when(c == 1)
        def _():
            positives_on(3)

    first_pass(0, False)
    positives_on(2)
    with_squares(first_passes)

    @pl.when(my_chunk > 0)
    def _():
        owner_terms()

    def second_pass(c, kept):
        await_chunk(c, WEIGHT, wdall)
        wt_ref[...] = twice(wdall[pl.ds(c * NO, NO)].reshape(NO * 8, 128))[:32, :]
        groups = JC if kept else JB

        def block(jb, carry):
            start = pl.multiple_of(jb * (8 * groups), 8 * groups)
            at = [pl.ds(start + 8 * v, 8) for v in range(groups)]
            acc = [zero] * groups
            for k in range(32):
                w = jnp.broadcast_to(wt_ref[k : k + 1, :], (8, 128))
                if not kept:
                    p = jnp.broadcast_to(pt_ref[c, k : k + 1, :], (8, 128))
                for v in range(groups):
                    if kept:
                        tt = squares[(c - 1) * 32 + k, at[v], :]
                    else:
                        t = jnp.tanh(st_ref[c, at[v], :] - p)
                        tt = t * t
                    acc[v] = acc[v] + w * (1.0 - tt)
            for v in range(groups):
                ct_ref[at[v], :] = acc[v]
            return carry

        lax.fori_loop(0, rows // (8 * groups), block, 0)
        hi, lo = [], []
        for a in range(nb):
            neg = jnp.transpose(ct_ref[a * 128 : a * 128 + 128, :])
            pos = []
            for i in range(NO):
                index = inv_ref[c * NO + i, :, a * 128 : a * 128 + 128]
                value = lane_gather(wdall[c * NO + i], jnp.bitwise_and(index, 127))
                pos.append(jnp.where(index >= 0, value, 0.0))
            cot = neg[:64, :] + neg[64:, :] + jnp.concatenate(pos, axis=0)
            top = cot.astype(BF16).astype(F32)
            hi.append(top)
            lo.append(cot - top)
        cot = jnp.concatenate([jnp.concatenate(hi, axis=1), jnp.concatenate(lo, axis=1)], axis=0)
        grad = dot_nn(cot.astype(BF16), mem_ref[...])
        gpart[pl.ds(c * NO, NO)] = (grad[:64, :] + grad[64:, :]).reshape(NO, 8, width)
        to_owners(c, gpart, grs, 6, GRAD, SPARE + 1)

    second_pass(0, False)
    with_squares(second_pass)

    grs[me] = gpart[my_place]
    await_blocks(recv_sem, GRAD + my_chunk, grs, n - 1)
    grad_ref[...] = jnp.sum(grs[0:n], axis=0)
    for i, buf in enumerate((rrs, grs)):
        await_blocks(recv_sem, SPARE + i, buf, 1)
    for send, buf, count in (
        (0, qall, n - 1), (1, tall, n - 1), (4, rpart, n), (5, wdall, n - 1), (6, gpart, n),
    ):
        await_blocks(send_sem, send, buf, count)
    for c in range(NC):
        await_blocks(send_sem, 2, pz.at[c], NZ - 1)
        await_blocks(send_sem, 3, py.at[c], NY - 1)


def on_device(n, queries, query_labels, positive_ids, positive_mask, memory, memory_labels):
    own, width = queries.shape
    rows = memory.shape[0]
    vmem = pl.BlockSpec(memory_space=pltpu.VMEM)
    smem = pl.BlockSpec(memory_space=pltpu.SMEM)
    return pl.pallas_call(
        functools.partial(kernel, n),
        out_shape=(
            jax.ShapeDtypeStruct((own,), F32),
            jax.ShapeDtypeStruct((own, width), F32),
        ),
        in_specs=[smem, vmem, vmem, vmem, vmem, pl.BlockSpec(memory_space=pltpu.HBM)],
        out_specs=(smem, vmem),
        scratch_shapes=[
            pltpu.VMEM((rows, width), BF16),
            pltpu.VMEM((own, 128), I32),
            pltpu.VMEM((own, 128), I16),
            pltpu.VMEM((n, own, width), BF16),
            pltpu.VMEM((n, own, 128), I16),
            pltpu.VMEM((n, own, 128), I32),
            pltpu.VMEM((NO * own, rows), F32),
            pltpu.VMEM((NC, rows, 128), F32),
            pltpu.VMEM((n, own, rows), I32),
            pltpu.VMEM((rows, 128), F32),
            pltpu.VMEM((NC, NO // 2, own, 128), F32),
            pltpu.VMEM((NC, NZ, NO // 2, own, 128), F32),
            pltpu.VMEM((NC, NO // 2, own, 128), F32),
            pltpu.VMEM((NC, NY, NO // 2, own, 128), F32),
            pltpu.VMEM((NC, NO // 2, own, 128), F32),
            pltpu.VMEM((NC, 32, 128), F32),
            pltpu.VMEM((own, 64, 128), F32),
            pltpu.VMEM((24, 128), F32),
            pltpu.VMEM((64, 8, 128), F32),
            pltpu.VMEM(((NC - 1) * 32, rows, 128), F32),
            pltpu.VMEM((n, own, 128), F32),
            pltpu.VMEM((n + 1, own, 128), F32),
            pltpu.VMEM((own, 128), F32),
            pltpu.VMEM((n, own, 128), F32),
            pltpu.VMEM((32, 128), F32),
            pltpu.VMEM((n, own, width), F32),
            pltpu.VMEM((n + 1, own, width), F32),
            pltpu.SemaphoreType.DMA((7,)),
            pltpu.SemaphoreType.DMA((N_RECV,)),
            pltpu.SemaphoreType.DMA,
        ],
        compiler_params=pltpu.CompilerParams(
            collective_id=0, has_side_effects=True, vmem_limit_bytes=VMEM_LIMIT
        ),
    )(
        query_labels, queries, positive_ids, positive_mask,
        memory_labels.reshape(rows // 128, 128), memory,
    )


def solution(mesh):
    n = mesh.shape["shard"]
    return jax.shard_map(
        functools.partial(on_device, n),
        mesh=mesh,
        in_specs=(
            P(("dp", "shard"), None),
            P(("dp", "shard")),
            P(("dp", "shard"), None),
            P(("dp", "shard"), None),
            P("shard", None),
            P("shard"),
        ),
        out_specs=(P(("dp", "shard")), P(("dp", "shard"), None)),
        check_vma=False,
    )
```

```python
import functools

import jax
import jax.numpy as jnp
from jax import lax
from jax.experimental import pallas as pl
from jax.experimental.pallas import tpu as pltpu
from jax.sharding import PartitionSpec as P

F32 = jnp.float32
BF16 = jnp.bfloat16
I32 = jnp.int32
I16 = jnp.int16
HALF_INV_TAU = 5.0
FAR = -1e6
MESH = pl.DeviceIdType.MESH
NY, NZ = 4, 8
NK, KB = 4, 8
G = 32
JC = 16
PIECES = 4
EARLY = (0, 2, 1)
VMEM_LIMIT = 60 * 1024 * 1024
DOWN, UP, RELAY, SIB, LAB, IN, TAB, POS, RANK, WEIGHT, GRAD, N_RECV = (
    0, 4, 8, 12, 15, 16, 17, 18, 19, 23, 27, 28,
)
S_MEM, S_LAB, S_IN, S_TAB, S_POS, S_RANK, S_WEIGHT, S_GRAD, N_SEND = range(9)


def dot_nt(a, b):
    return lax.dot_general(a, b, (((1,), (1,)), ((), ())), preferred_element_type=F32)


def dot_nn(a, b):
    return lax.dot_general(a, b, (((1,), (0,)), ((), ())), preferred_element_type=F32)


def lane_gather(table, index):
    return jnp.take_along_axis(table, index, axis=1, mode="promise_in_bounds")


def twice(x):
    return jnp.transpose(jnp.concatenate([x, pltpu.roll(x, 96, axis=1)], axis=0))


def columns(x):
    return jnp.transpose(jnp.concatenate([x] * 16, axis=0))


def kernel(
    lab_ref, q_ref, id_ref, mask_ref, mlab_ref, mem_hbm, prec_ref, grad_ref,
    mem_ref, labs, tab_ref, half_ref, qall, tall, idall, s_ref, st_ref, inv_ref, ct_ref,
    ppart, pz, pt_ref, wq_ref, aux_ref,
    racc, squares, rpart, rrs, ranks, wdown, wdall, wt_ref, gacc, gpart, grs,
    send_sem, recv_sem, mem_sem,
):
    dp = lax.axis_index("dp")
    me = lax.axis_index("shard")
    block_rows, width = mem_hbm.shape
    nb = block_rows // 128
    rows = NY * block_rows
    core = lax.rem(dp, 2)
    sibling = {"dp": dp + 1 - 2 * core, "shard": me}
    my_y, my_z = lax.div(me, NZ), lax.rem(me, NZ)
    y_at = [lax.rem(my_y + d, NY) for d in range(NY)]
    z_at = [lax.rem(my_z + d, NZ) for d in range(NZ)]
    along_z = [{"shard": my_y * NZ + z_at[d]} for d in range(NZ)]
    along_y = [{"shard": y_at[d] * NZ + my_z} for d in range(NY)]
    far_first = (4, 3, 5, 2, 6, 1, 7)

    barrier = pltpu.get_barrier_semaphore()
    for peer in [along_z[d] for d in far_first] + [along_y[d] for d in (2, 1, 3)] + [sibling]:
        pl.semaphore_signal(barrier, inc=1, device_id=peer, device_id_type=MESH)

    load_memory = pltpu.make_async_copy(mem_hbm, mem_ref.at[my_y], mem_sem)
    load_memory.start()

    row = lax.broadcasted_iota(I32, (8, 64), 0)
    label = jnp.zeros((8, 64), I32)
    for i in range(8):
        label = jnp.where(row == i, lab_ref[i], label)
    tab_ref[:, 0:64] = jnp.where(mask_ref[...] > 0, id_ref[...], -1)
    tab_ref[:, 64:128] = label
    half_ref[...] = tab_ref[...].astype(I16)
    qall[my_z] = q_ref[...]
    tall[my_z] = half_ref[...]
    labs[my_y] = mlab_ref[...]

    def put(src, dst, send, recv, peer):
        pltpu.make_async_remote_copy(
            src_ref=src, dst_ref=dst, send_sem=send_sem.at[send], recv_sem=recv_sem.at[recv],
            device_id=peer, device_id_type=MESH,
        ).start()

    def await_bytes(sem, index, view):
        pltpu.make_async_copy(view, view, sem.at[index]).wait()

    def await_line(recv, buf):
        await_bytes(recv_sem, recv, buf.at[pl.ds(0, NZ - 1)])

    def to_line(src, dst, send, recv):
        for d in far_first:
            put(src.at[z_at[d]], dst.at[my_z], send, recv, along_z[d])

    def on_line(src, dst, send, recv):
        for d in far_first:
            put(src, dst.at[my_z], send, recv, along_z[d])

    def part(piece):
        return pl.ds(pl.multiple_of(core * (block_rows // 2) + piece * 128, 128), 128)

    def hand_on(block, piece, recv):
        view = mem_ref.at[block, part(piece)]
        put(view, view, S_MEM, recv, sibling)

    pl.semaphore_wait(barrier, NZ + NY - 1)
    on_line(half_ref, tall, S_TAB, TAB)
    on_line(q_ref, qall, S_IN, IN)
    for up_piece, down_piece in ((0, 2), (1, 3), (2, 0), (3, 1)):
        for piece, recv, peer in ((up_piece, DOWN, along_y[1]), (down_piece, UP, along_y[3])):
            put(mem_hbm.at[part(piece)], mem_ref.at[my_y, part(piece)], S_MEM, recv + piece, peer)
    for d in (2, 1, 3):
        put(mlab_ref, labs.at[my_y], S_LAB, LAB, along_y[d])

    def landed(block, piece, recv):
        await_bytes(recv_sem, recv + piece, mem_ref.at[block, part(piece)])

    for step in range(2):
        piece = step
        landed(y_at[3], piece, DOWN)
        view = mem_ref.at[y_at[3], part(piece)]
        put(view, view, S_MEM, RELAY + piece, along_y[1])
        hand_on(y_at[3], piece, SIB)
        piece = step + 2
        landed(y_at[1], piece, UP)
        view = mem_ref.at[y_at[1], part(piece)]
        put(view, view, S_MEM, RELAY + piece, along_y[3])
        hand_on(y_at[1], piece, SIB + 1)

    await_line(TAB, tall)
    lane = lax.broadcasted_iota(I32, (8, 128), 1)
    for i in range(NZ):
        idall[i] = tall[i].astype(I32)

    def invert(b, y):
        local = idall[b] - (y * NZ + my_z) * block_rows
        found = [jnp.full((8, 128), -1, I32) for _ in range(nb)]
        for k in range(64):
            here = jnp.broadcast_to(local[:, k : k + 1], (8, 128))
            for a in range(nb):
                found[a] = jnp.where(here == lane + a * 128, 64 + k, found[a])
        for a in range(nb):
            inv_ref[b, y * nb + a] = found[a]
        return y

    def invert_owner(b):
        def one(y, c):
            invert(b, y)
            return c

        lax.fori_loop(0, NY, one, 0)

    owner = iter(range(NZ))
    for step in range(2):
        piece = step + 2
        landed(y_at[3], piece, DOWN)
        hand_on(y_at[3], piece, SIB)
        invert_owner(next(owner))
        piece = step
        landed(y_at[1], piece, UP)
        hand_on(y_at[1], piece, SIB + 1)
        invert_owner(next(owner))
    for piece in (0, 2, 1, 3):
        landed(y_at[2], piece, RELAY)
        hand_on(y_at[2], piece, SIB + 2)
        if piece in EARLY:
            invert_owner(next(owner))

    await_line(IN, qall)
    load_memory.wait()
    queries = jnp.concatenate([qall[i].astype(F32) for i in range(NZ)], axis=0).astype(BF16)
    for step, (d, arrived) in enumerate(((0, None), (3, SIB), (1, SIB + 1), (2, SIB + 2))):
        y = y_at[d]
        if arrived is not None:
            await_bytes(recv_sem, arrived, mem_ref.at[y, pl.ds(0, block_rows // 2)])
        s_ref[...] = dot_nt(queries, mem_ref[y])
        for i in range(NZ // 2):
            pair = None
            for j in (i, i + NZ // 2):
                local = idall[j] - (y * NZ + my_z) * block_rows
                place = jnp.bitwise_and(local, 127)
                which = jnp.right_shift(local, 7)
                value = jnp.zeros((8, 128), F32)
                for a in range(nb):
                    block = s_ref[j * 8 : j * 8 + 8, a * 128 : a * 128 + 128]
                    value = jnp.where(which == a, lane_gather(block, place), value)
                value = jnp.where(lane < 64, value * HALF_INV_TAU, 0.0)
                pair = value if pair is None else pair + pltpu.roll(value, 64, axis=1)
            ppart[i] = pair if step == 0 else ppart[i] + pair
    on_line(ppart, pz, S_POS, POS)
    pz[my_z] = ppart[...]

    for b in owner:
        invert_owner(b)
    await_bytes(recv_sem, LAB, labs.at[pl.ds(0, NY - 1)])
    queries = jnp.concatenate([queries, queries], axis=0)
    ids = idall[...].reshape(NZ * 8, 128)
    labels = jnp.transpose(jnp.concatenate([ids, ids], axis=0))[64:65, :]

    def score(y, c):
        lab_t = columns(labs[y])
        for a in range(nb):
            st = dot_nt(mem_ref[y, a * 128 : a * 128 + 128, :], queries) * HALF_INV_TAU
            column = jnp.broadcast_to(lab_t[:, a : a + 1], (128, 128))
            st_ref[pl.ds(pl.multiple_of(y * block_rows + a * 128, 128), 128), :] = jnp.where(
                column != labels, st, FAR
            )
        return c

    lax.fori_loop(0, NY, score, 0)

    await_line(POS, pz)
    pos = jnp.sum(pz[...], axis=0)
    half_line = NZ // 2
    own = jnp.where(lane < 64, pos[0], 0.0)
    for i in range(1, NZ):
        block = pos[i % half_line]
        block = pltpu.roll(block, 64, axis=1) if i >= half_line else block
        own = jnp.where(jnp.logical_and(my_z == i, lane < 64), block, own)
    pos = pos.reshape(half_line * 8, 128)
    pt_ref[...] = twice(jnp.concatenate([pos, pltpu.roll(pos, 64, axis=1)], axis=0))[:32, :]
    zero = jnp.zeros((8, 128), F32)
    mask = jnp.where(jnp.logical_and(lane < 64, tab_ref[...] >= 0), 1.0, 0.0)
    found = jnp.sum(mask, axis=1, keepdims=True)

    def first_pass(c):
        p = [jnp.broadcast_to(pt_ref[c * KB + i : c * KB + i + 1, :], (8, 128)) for i in range(KB)]

        def step(g, acc):
            acc = list(acc)
            at = [pl.ds(pl.multiple_of(g * (8 * G), 8 * G) + 8 * v, 8) for v in range(G)]
            for i in range(KB):
                one = two = None
                for v in range(G):
                    t = jnp.tanh(st_ref[at[v], :] - p[i])
                    tt = t * t
                    if c:
                        squares[(c - 1) * KB + i, at[v], :] = tt
                    one = t if one is None else one + t
                    two = tt if two is None else two + tt
                acc[2 * i] = acc[2 * i] + (one + float(G))
                acc[2 * i + 1] = acc[2 * i + 1] + (float(G) - two)
            return tuple(acc)

        acc = lax.fori_loop(0, rows // (8 * G), step, (zero,) * (2 * KB), unroll=2)
        for i in range(KB):
            racc[i] = acc[2 * i]
            racc[KB + i] = acc[2 * i + 1]
        sums = jnp.sum(racc[...], axis=1)
        spread = [jnp.zeros((8, 128), F32)] * 16
        spread[c] = 0.5 * sums[:KB, :]
        spread[8 + c] = 0.25 * sums[KB:, :]
        both = jnp.transpose(jnp.concatenate(spread, axis=0))
        both = both[:64, :] + pltpu.roll(both[64:, :], 32, axis=1)
        rpart[c] = both.reshape(NZ, 8, 128)
        to_line(rpart.at[c], rrs.at[c], S_RANK, RANK + c)
        rrs[c, my_z] = rpart[c, my_z]

    def positive_terms():
        own_t = columns(own)
        mask_t = columns(mask)
        off = jnp.where(
            lax.broadcasted_iota(I32, (64, 128), 0) == lax.broadcasted_iota(I32, (64, 128), 1),
            0.0, 1.0,
        )
        for i in range(8):
            col = jnp.broadcast_to(own_t[:64, i : i + 1], (64, 128))
            mcol = jnp.broadcast_to(mask_t[:64, i : i + 1], (64, 128)) * off
            t = jnp.tanh(col - own[i : i + 1, :])
            w = (1.0 - t * t) * (0.25 * off)
            wq_ref[i] = w
            aux_ref[i : i + 1, :] = 1.0 + jnp.sum(mcol * (0.5 + 0.5 * t), axis=0, keepdims=True)
            aux_ref[8 + i : 9 + i, :] = jnp.sum(mcol * w, axis=0, keepdims=True)

    def owner_terms(c):
        await_line(RANK + c, rrs.at[c])
        rank_neg = jnp.sum(rrs[c], axis=0)
        if c:
            rank_neg = rank_neg + ranks[...]
        ranks[...] = rank_neg
        rank_pos = aux_ref[0:8, :]
        total = rank_pos + rank_neg
        share = mask / (found * total * total)
        weight_neg = share * rank_pos
        both = jnp.where(lane < 64, weight_neg * (0.5 * HALF_INV_TAU), 0.0)
        if c == NK - 1:
            slope_neg = pltpu.roll(rank_neg, 64, axis=1)
            spread = aux_ref[8:16, :]
            weight_pos = -share * rank_neg
            wp_t = columns(weight_pos)
            for i in range(8):
                col = jnp.broadcast_to(wp_t[:64, i : i + 1], (64, 128))
                aux_ref[16 + i : 17 + i, :] = jnp.sum(col * wq_ref[i], axis=0, keepdims=True)
            backed = aux_ref[16:24, :]
            dpos = mask * backed - weight_neg * slope_neg - weight_pos * spread
            dpos = pltpu.roll(dpos * (2.0 * HALF_INV_TAU), 64, axis=1)
            both = jnp.where(lane < 64, both, dpos)
        wdown[c] = both
        on_line(wdown.at[c], wdall.at[c], S_WEIGHT, WEIGHT + c)
        wdall[c, my_z] = both
        if c == NK - 1:
            precision = jnp.sum(mask * rank_pos / total, axis=1, keepdims=True) / found
            for i in range(8):
                prec_ref[i] = precision[i, 0]

    def weigh(c, at, acc):
        for i in range(KB):
            w = jnp.broadcast_to(wt_ref[c * KB + i : c * KB + i + 1, :], (8, 128))
            if not c:
                p = jnp.broadcast_to(pt_ref[i : i + 1, :], (8, 128))
            for v in range(len(at)):
                if c:
                    tt = squares[(c - 1) * KB + i, at[v], :]
                else:
                    t = jnp.tanh(st_ref[at[v], :] - p)
                    tt = t * t
                acc[v] = acc[v] + w * (1.0 - tt)
        return acc

    def await_weights(c):
        await_line(WEIGHT + c, wdall.at[c])
        weights = twice(wdall[c].reshape(NZ * 8, 128))
        wt_ref[c * KB : c * KB + KB, :] = weights[c * KB : c * KB + KB, :]

    def second_pass(c):
        await_weights(c)

        def block(jb, carry):
            start = pl.multiple_of(jb * (8 * JC), 8 * JC)
            at = [pl.ds(start + 8 * v, 8) for v in range(JC)]
            acc = weigh(c, at, [ct_ref[at[v], :] if c else zero for v in range(JC)])
            for v in range(JC):
                ct_ref[at[v], :] = acc[v]
            return carry

        lax.fori_loop(0, rows // (8 * JC), block, 0, unroll=2)

    def last_pass(c):
        await_weights(c)
        gacc[...] = jnp.zeros_like(gacc)

        def block(a, carry):
            start = pl.multiple_of(a * 128, 128)
            at = [pl.ds(start + 8 * v, 8) for v in range(16)]
            acc = weigh(c, at, [ct_ref[at[v], :] for v in range(16)])
            neg = jnp.transpose(jnp.concatenate(acc, axis=0))
            pos = []
            for i in range(NZ):
                index = inv_ref[i, a]
                value = lane_gather(wdall[c, i], jnp.bitwise_and(index, 127))
                pos.append(jnp.where(index >= 0, value, 0.0))
            cot = neg[:64, :] + neg[64:, :] + jnp.concatenate(pos, axis=0)
            top = cot.astype(BF16).astype(F32)
            cot = jnp.concatenate([top, cot - top], axis=0).astype(BF16)
            memory = mem_ref[lax.div(a, nb), pl.ds(pl.multiple_of(lax.rem(a, nb) * 128, 128), 128), :]
            gacc[...] = gacc[...] + dot_nn(cot, memory)
            return carry

        lax.fori_loop(0, rows // 128, block, 0, unroll=2)
        grad = gacc[...]
        gpart[...] = (grad[:64, :] + grad[64:, :]).reshape(NZ, 8, width)
        to_line(gpart, grs, S_GRAD, GRAD)
        grs[my_z] = gpart[my_z]

    first_pass(0)
    first_pass(1)
    positive_terms()
    first_pass(2)
    owner_terms(0)
    first_pass(3)
    owner_terms(1)
    owner_terms(2)
    second_pass(0)
    owner_terms(3)
    second_pass(1)
    second_pass(2)
    last_pass(3)

    await_line(GRAD, grs)
    grad_ref[...] = jnp.sum(grs[...], axis=0)
    await_bytes(send_sem, S_MEM, mem_ref.at[pl.ds(0, 3)])
    await_bytes(send_sem, S_LAB, labs.at[pl.ds(0, NY - 1)])
    for send, buf in ((S_IN, qall), (S_TAB, tall), (S_POS, pz), (S_GRAD, grs)):
        await_bytes(send_sem, send, buf.at[pl.ds(0, NZ - 1)])
    for c in range(NK):
        await_bytes(send_sem, S_RANK, rrs.at[c, pl.ds(0, NZ - 1)])
        await_bytes(send_sem, S_WEIGHT, wdall.at[c, pl.ds(0, NZ - 1)])


def on_device(queries, query_labels, positive_ids, positive_mask, memory, memory_labels):
    own, width = queries.shape
    rows = memory.shape[0]
    vmem = pl.BlockSpec(memory_space=pltpu.VMEM)
    smem = pl.BlockSpec(memory_space=pltpu.SMEM)
    return pl.pallas_call(
        kernel,
        out_shape=(
            jax.ShapeDtypeStruct((own,), F32),
            jax.ShapeDtypeStruct((own, width), F32),
        ),
        in_specs=[smem, vmem, vmem, vmem, vmem, pl.BlockSpec(memory_space=pltpu.HBM)],
        out_specs=(smem, vmem),
        scratch_shapes=[
            pltpu.VMEM((NY, rows, width), BF16),
            pltpu.VMEM((NY, rows // 128, 128), I32),
            pltpu.VMEM((own, 128), I32),
            pltpu.VMEM((own, 128), I16),
            pltpu.VMEM((NZ, own, width), BF16),
            pltpu.VMEM((NZ, own, 128), I16),
            pltpu.VMEM((NZ, own, 128), I32),
            pltpu.VMEM((NZ * own, rows), F32),
            pltpu.VMEM((NY * rows, 128), F32),
            pltpu.VMEM((NZ, NY * rows // 128, own, 128), I32),
            pltpu.VMEM((NY * rows, 128), F32),
            pltpu.VMEM((NZ // 2, own, 128), F32),
            pltpu.VMEM((NZ, NZ // 2, own, 128), F32),
            pltpu.VMEM((32, 128), F32),
            pltpu.VMEM((own, 64, 128), F32),
            pltpu.VMEM((24, 128), F32),
            pltpu.VMEM((2 * KB, 8, 128), F32),
            pltpu.VMEM(((NK - 1) * KB, NY * rows, 128), F32),
            pltpu.VMEM((NK, NZ, own, 128), F32),
            pltpu.VMEM((NK, NZ, own, 128), F32),
            pltpu.VMEM((own, 128), F32),
            pltpu.VMEM((NK, own, 128), F32),
            pltpu.VMEM((NK, NZ, own, 128), F32),
            pltpu.VMEM((32, 128), F32),
            pltpu.VMEM((2 * NZ * own, width), F32),
            pltpu.VMEM((NZ, own, width), F32),
            pltpu.VMEM((NZ, own, width), F32),
            pltpu.SemaphoreType.DMA((N_SEND,)),
            pltpu.SemaphoreType.DMA((N_RECV,)),
            pltpu.SemaphoreType.DMA,
        ],
        compiler_params=pltpu.CompilerParams(
            collective_id=0, has_side_effects=True, vmem_limit_bytes=VMEM_LIMIT
        ),
    )(
        query_labels, queries, positive_ids, positive_mask,
        memory_labels.reshape(rows // 128, 128), memory,
    )


def solution(mesh):
    return jax.shard_map(
        on_device,
        mesh=mesh,
        in_specs=(
            P(("dp", "shard"), None),
            P(("dp", "shard")),
            P(("dp", "shard"), None),
            P(("dp", "shard"), None),
            P("shard", None),
            P("shard"),
        ),
        out_specs=(P(("dp", "shard")), P(("dp", "shard"), None)),
        check_vma=False,
    )
```

```python
import functools

import jax
import jax.numpy as jnp
from jax import lax
from jax.experimental import pallas as pl
from jax.experimental.pallas import tpu as pltpu
from jax.sharding import PartitionSpec as P

F32 = jnp.float32
BF16 = jnp.bfloat16
I32 = jnp.int32
I16 = jnp.int16
HALF_INV_TAU = 5.0
FAR = -1e6
MESH = pl.DeviceIdType.MESH
NY, NZ = 4, 8
NK, KB = 4, 8
G = 32
JC = 16
PIECES = 4
EARLY = ()
VMEM_LIMIT = 67_043_328 - 327_680
DOWN, UP, RELAY, SIB, LAB, IN, TAB, POS, RANK, WEIGHT, GRAD, N_RECV = (
    0, 4, 8, 12, 15, 16, 17, 18, 19, 23, 27, 28,
)
S_MEM, S_LAB, S_IN, S_TAB, S_POS, S_RANK, S_WEIGHT, S_GRAD, N_SEND = range(9)


def dot_nt(a, b):
    return lax.dot_general(a, b, (((1,), (1,)), ((), ())), preferred_element_type=F32)


def dot_nn(a, b):
    return lax.dot_general(a, b, (((1,), (0,)), ((), ())), preferred_element_type=F32)


def lane_gather(table, index):
    return jnp.take_along_axis(table, index, axis=1, mode="promise_in_bounds")


def twice(x):
    return jnp.transpose(jnp.concatenate([x, pltpu.roll(x, 96, axis=1)], axis=0))


def columns(x):
    return jnp.transpose(jnp.concatenate([x] * 16, axis=0))


def kernel(
    lab_ref, q_ref, id_ref, mask_ref, mlab_ref, mem_hbm, prec_ref, grad_ref,
    mem_ref, labs, tab_ref, half_ref, qall, tall, idall, s_ref, st_ref, inv_ref, ct_ref,
    ppart, pz, pt_ref, wq_ref, aux_ref,
    racc, squares, rpart, rrs, ranks, wdown, wdall, wt_ref, memt_ref, cneg_ref, cpos_ref, gpart, grs,
    send_sem, recv_sem, mem_sem,
):
    dp = lax.axis_index("dp")
    me = lax.axis_index("shard")
    block_rows, width = mem_hbm.shape
    nb = block_rows // 128
    rows = NY * block_rows
    core = lax.rem(dp, 2)
    sibling = {"dp": dp + 1 - 2 * core, "shard": me}
    my_y, my_z = lax.div(me, NZ), lax.rem(me, NZ)
    y_at = [lax.rem(my_y + d, NY) for d in range(NY)]
    z_at = [lax.rem(my_z + d, NZ) for d in range(NZ)]
    along_z = [{"shard": my_y * NZ + z_at[d]} for d in range(NZ)]
    along_y = [{"shard": y_at[d] * NZ + my_z} for d in range(NY)]
    far_first = (4, 3, 5, 2, 6, 1, 7)

    barrier = pltpu.get_barrier_semaphore()
    for peer in [along_z[d] for d in far_first] + [along_y[d] for d in (2, 1, 3)] + [sibling]:
        pl.semaphore_signal(barrier, inc=1, device_id=peer, device_id_type=MESH)

    load_memory = pltpu.make_async_copy(mem_hbm, mem_ref.at[my_y], mem_sem)
    load_memory.start()

    row = lax.broadcasted_iota(I32, (8, 64), 0)
    label = jnp.zeros((8, 64), I32)
    for i in range(8):
        label = jnp.where(row == i, lab_ref[i], label)
    tab_ref[:, 0:64] = jnp.where(mask_ref[...] > 0, id_ref[...], -1)
    tab_ref[:, 64:128] = label
    half_ref[...] = tab_ref[...].astype(I16)
    qall[my_z] = q_ref[...]
    tall[my_z] = half_ref[...]
    labs[my_y] = mlab_ref[...]

    def put(src, dst, send, recv, peer):
        pltpu.make_async_remote_copy(
            src_ref=src, dst_ref=dst, send_sem=send_sem.at[send], recv_sem=recv_sem.at[recv],
            device_id=peer, device_id_type=MESH,
        ).start()

    def await_bytes(sem, index, view):
        pltpu.make_async_copy(view, view, sem.at[index]).wait()

    def await_line(recv, buf):
        await_bytes(recv_sem, recv, buf.at[pl.ds(0, NZ - 1)])

    def to_line(src, dst, send, recv):
        for d in far_first:
            put(src.at[z_at[d]], dst.at[my_z], send, recv, along_z[d])

    def on_line(src, dst, send, recv):
        for d in far_first:
            put(src, dst.at[my_z], send, recv, along_z[d])

    def part(piece):
        return pl.ds(pl.multiple_of(core * (block_rows // 2) + piece * 128, 128), 128)

    def hand_on(block, piece, recv):
        view = mem_ref.at[block, part(piece)]
        put(view, view, S_MEM, recv, sibling)

    pl.semaphore_wait(barrier, NZ + NY - 1)
    on_line(half_ref, tall, S_TAB, TAB)
    on_line(q_ref, qall, S_IN, IN)
    for up_piece, down_piece in ((0, 2), (1, 3), (2, 0), (3, 1)):
        for piece, recv, peer in ((up_piece, DOWN, along_y[1]), (down_piece, UP, along_y[3])):
            put(mem_hbm.at[part(piece)], mem_ref.at[my_y, part(piece)], S_MEM, recv + piece, peer)
    for d in (2, 1, 3):
        put(mlab_ref, labs.at[my_y], S_LAB, LAB, along_y[d])

    def landed(block, piece, recv):
        await_bytes(recv_sem, recv + piece, mem_ref.at[block, part(piece)])

    for step in range(2):
        piece = step
        landed(y_at[3], piece, DOWN)
        view = mem_ref.at[y_at[3], part(piece)]
        put(view, view, S_MEM, RELAY + piece, along_y[1])
        hand_on(y_at[3], piece, SIB)
        piece = step + 2
        landed(y_at[1], piece, UP)
        view = mem_ref.at[y_at[1], part(piece)]
        put(view, view, S_MEM, RELAY + piece, along_y[3])
        hand_on(y_at[1], piece, SIB + 1)

    await_line(TAB, tall)
    lane = lax.broadcasted_iota(I32, (8, 128), 1)
    for i in range(NZ):
        idall[i] = tall[i].astype(I32)

    def invert(b, y):
        local = idall[b] - (y * NZ + my_z) * block_rows
        found = [jnp.full((8, 128), -1, I32) for _ in range(nb)]
        for k in range(64):
            here = jnp.broadcast_to(local[:, k : k + 1], (8, 128))
            for a in range(nb):
                found[a] = jnp.where(here == lane + a * 128, 64 + k, found[a])
        for a in range(nb):
            inv_ref[b, y * nb + a] = found[a]
        return y

    def invert_owner(b):
        def one(y, c):
            invert(b, y)
            return c

        lax.fori_loop(0, NY, one, 0)

    owner = iter(range(NZ))
    for step in range(2):
        piece = step + 2
        landed(y_at[3], piece, DOWN)
        hand_on(y_at[3], piece, SIB)
        invert_owner(next(owner))
        piece = step
        landed(y_at[1], piece, UP)
        hand_on(y_at[1], piece, SIB + 1)
        invert_owner(next(owner))
    for piece in (0, 2, 1, 3):
        landed(y_at[2], piece, RELAY)
        hand_on(y_at[2], piece, SIB + 2)
        if piece in EARLY:
            invert_owner(next(owner))

    await_line(IN, qall)
    load_memory.wait()
    queries = jnp.concatenate([qall[i].astype(F32) for i in range(NZ)], axis=0).astype(BF16)
    for step, (d, arrived) in enumerate(((0, None), (3, SIB), (1, SIB + 1), (2, SIB + 2))):
        y = y_at[d]
        if arrived is not None:
            await_bytes(recv_sem, arrived, mem_ref.at[y, pl.ds(0, block_rows // 2)])
        s_ref[...] = dot_nt(queries, mem_ref[y])
        for i in range(NZ // 2):
            pair = None
            for j in (i, i + NZ // 2):
                local = idall[j] - (y * NZ + my_z) * block_rows
                place = jnp.bitwise_and(local, 127)
                which = jnp.right_shift(local, 7)
                value = jnp.zeros((8, 128), F32)
                for a in range(nb):
                    block = s_ref[j * 8 : j * 8 + 8, a * 128 : a * 128 + 128]
                    value = jnp.where(which == a, lane_gather(block, place), value)
                value = jnp.where(lane < 64, value * HALF_INV_TAU, 0.0)
                pair = value if pair is None else pair + pltpu.roll(value, 64, axis=1)
            ppart[i] = pair if step == 0 else ppart[i] + pair
    on_line(ppart, pz, S_POS, POS)
    pz[my_z] = ppart[...]

    for _ in range(2):
        invert_owner(next(owner))
    await_bytes(recv_sem, LAB, labs.at[pl.ds(0, NY - 1)])
    queries = jnp.concatenate([queries, queries], axis=0)
    ids = idall[...].reshape(NZ * 8, 128)
    labels = jnp.transpose(jnp.concatenate([ids, ids], axis=0))[64:65, :]

    def score(y, c):
        lab_t = columns(labs[y])
        for a in range(nb):
            st = dot_nt(mem_ref[y, a * 128 : a * 128 + 128, :], queries) * HALF_INV_TAU
            column = jnp.broadcast_to(lab_t[:, a : a + 1], (128, 128))
            st_ref[pl.ds(pl.multiple_of(y * block_rows + a * 128, 128), 128), :] = jnp.where(
                column != labels, st, FAR
            )
            flipped = jnp.transpose(mem_ref[y, a * 128 : a * 128 + 128, :].astype(F32))
            memt_ref[:, pl.ds(pl.multiple_of(y * block_rows + a * 128, 128), 128)] = flipped.astype(BF16)
        return c

    lax.fori_loop(0, NY, score, 0)

    await_line(POS, pz)
    pos = jnp.sum(pz[...], axis=0)
    half_line = NZ // 2
    own = jnp.where(lane < 64, pos[0], 0.0)
    for i in range(1, NZ):
        block = pos[i % half_line]
        block = pltpu.roll(block, 64, axis=1) if i >= half_line else block
        own = jnp.where(jnp.logical_and(my_z == i, lane < 64), block, own)
    pos = pos.reshape(half_line * 8, 128)
    pt_ref[...] = twice(jnp.concatenate([pos, pltpu.roll(pos, 64, axis=1)], axis=0))[:32, :]
    zero = jnp.zeros((8, 128), F32)
    mask = jnp.where(jnp.logical_and(lane < 64, tab_ref[...] >= 0), 1.0, 0.0)
    found = jnp.sum(mask, axis=1, keepdims=True)

    def first_pass(c):
        p = [jnp.broadcast_to(pt_ref[c * KB + i : c * KB + i + 1, :], (8, 128)) for i in range(KB)]

        def step(g, acc):
            acc = list(acc)
            at = [pl.ds(pl.multiple_of(g * (8 * G), 8 * G) + 8 * v, 8) for v in range(G)]
            for i in range(KB):
                one = two = None
                for v in range(G):
                    t = jnp.tanh(st_ref[at[v], :] - p[i])
                    tt = t * t
                    if c:
                        squares[(c - 1) * KB + i, at[v], :] = tt
                    one = t if one is None else one + t
                    two = tt if two is None else two + tt
                acc[2 * i] = acc[2 * i] + (one + float(G))
                acc[2 * i + 1] = acc[2 * i + 1] + (float(G) - two)
            return tuple(acc)

        acc = lax.fori_loop(0, rows // (8 * G), step, (zero,) * (2 * KB), unroll=2)
        for i in range(KB):
            racc[i] = acc[2 * i]
            racc[KB + i] = acc[2 * i + 1]
        sums = jnp.sum(racc[...], axis=1)
        spread = [jnp.zeros((8, 128), F32)] * 16
        spread[c] = 0.5 * sums[:KB, :]
        spread[8 + c] = 0.25 * sums[KB:, :]
        both = jnp.transpose(jnp.concatenate(spread, axis=0))
        both = both[:64, :] + pltpu.roll(both[64:, :], 32, axis=1)
        rpart[c] = both.reshape(NZ, 8, 128)
        to_line(rpart.at[c], rrs.at[c], S_RANK, RANK + c)
        rrs[c, my_z] = rpart[c, my_z]

    def positive_terms():
        own_t = columns(own)
        mask_t = columns(mask)
        off = jnp.where(
            lax.broadcasted_iota(I32, (64, 128), 0) == lax.broadcasted_iota(I32, (64, 128), 1),
            0.0, 1.0,
        )
        for i in range(8):
            col = jnp.broadcast_to(own_t[:64, i : i + 1], (64, 128))
            mcol = jnp.broadcast_to(mask_t[:64, i : i + 1], (64, 128)) * off
            t = jnp.tanh(col - own[i : i + 1, :])
            w = (1.0 - t * t) * (0.25 * off)
            wq_ref[i] = w
            aux_ref[i : i + 1, :] = 1.0 + jnp.sum(mcol * (0.5 + 0.5 * t), axis=0, keepdims=True)
            aux_ref[8 + i : 9 + i, :] = jnp.sum(mcol * w, axis=0, keepdims=True)

    def owner_terms(c):
        await_line(RANK + c, rrs.at[c])
        rank_neg = jnp.sum(rrs[c], axis=0)
        if c:
            rank_neg = rank_neg + ranks[...]
        ranks[...] = rank_neg
        rank_pos = aux_ref[0:8, :]
        total = rank_pos + rank_neg
        share = mask / (found * total * total)
        weight_neg = share * rank_pos
        both = jnp.where(lane < 64, weight_neg * (0.5 * HALF_INV_TAU), 0.0)
        if c == NK - 1:
            slope_neg = pltpu.roll(rank_neg, 64, axis=1)
            spread = aux_ref[8:16, :]
            weight_pos = -share * rank_neg
            wp_t = columns(weight_pos)
            for i in range(8):
                col = jnp.broadcast_to(wp_t[:64, i : i + 1], (64, 128))
                aux_ref[16 + i : 17 + i, :] = jnp.sum(col * wq_ref[i], axis=0, keepdims=True)
            backed = aux_ref[16:24, :]
            dpos = mask * backed - weight_neg * slope_neg - weight_pos * spread
            dpos = pltpu.roll(dpos * (2.0 * HALF_INV_TAU), 64, axis=1)
            both = jnp.where(lane < 64, both, dpos)
        wdown[c] = both
        on_line(wdown.at[c], wdall.at[c], S_WEIGHT, WEIGHT + c)
        wdall[c, my_z] = both
        if c == NK - 1:
            precision = jnp.sum(mask * rank_pos / total, axis=1, keepdims=True) / found
            for i in range(8):
                prec_ref[i] = precision[i, 0]

    def weigh(c, at, acc):
        for i in range(KB):
            w = jnp.broadcast_to(wt_ref[c * KB + i : c * KB + i + 1, :], (8, 128))
            if not c:
                p = jnp.broadcast_to(pt_ref[i : i + 1, :], (8, 128))
            for v in range(len(at)):
                if c:
                    tt = squares[(c - 1) * KB + i, at[v], :]
                else:
                    t = jnp.tanh(st_ref[at[v], :] - p)
                    tt = t * t
                acc[v] = acc[v] + w * (1.0 - tt)
        return acc

    def await_weights(c):
        await_line(WEIGHT + c, wdall.at[c])
        weights = twice(wdall[c].reshape(NZ * 8, 128))
        wt_ref[c * KB : c * KB + KB, :] = weights[c * KB : c * KB + KB, :]

    def second_pass(c):
        await_weights(c)

        def block(jb, carry):
            start = pl.multiple_of(jb * (8 * JC), 8 * JC)
            at = [pl.ds(start + 8 * v, 8) for v in range(JC)]
            acc = weigh(c, at, [ct_ref[at[v], :] if c else zero for v in range(JC)])
            for v in range(JC):
                ct_ref[at[v], :] = acc[v]
            return carry

        lax.fori_loop(0, rows // (8 * JC), block, 0, unroll=2)

    def last_pass(c):
        await_weights(c)
        def block(a, carry):
            start = pl.multiple_of(a * 128, 128)
            at = [pl.ds(start + 8 * v, 8) for v in range(16)]
            acc = weigh(c, at, [ct_ref[at[v], :] for v in range(16)])
            neg = jnp.concatenate(acc, axis=0)
            top = neg.astype(BF16)
            cneg_ref[pl.ds(start, 128), 0:128] = top
            cneg_ref[pl.ds(start, 128), 128:256] = (neg - top.astype(F32)).astype(BF16)
            pos = []
            for i in range(NZ):
                index = inv_ref[i, a]
                value = lane_gather(wdall[c, i], jnp.bitwise_and(index, 127))
                pos.append(jnp.where(index >= 0, value, 0.0))
            pos = jnp.concatenate(pos, axis=0)
            top = pos.astype(BF16)
            cpos_ref[0:64, pl.ds(start, 128)] = top
            cpos_ref[64:128, pl.ds(start, 128)] = (pos - top.astype(F32)).astype(BF16)
            return carry

        lax.fori_loop(0, rows // 128, block, 0, unroll=4)
        neg = pos = None
        for y in range(NY):
            span = slice(y * block_rows, (y + 1) * block_rows)
            one = dot_nn(memt_ref[:, span], cneg_ref[span, :])
            two = dot_nn(cpos_ref[:, span], mem_ref[y])
            neg = one if neg is None else neg + one
            pos = two if pos is None else pos + two
        neg = jnp.transpose(neg[:, :128] + neg[:, 128:])
        grad = neg[:64, :] + neg[64:, :] + pos[:64, :] + pos[64:, :]
        gpart[...] = grad.reshape(NZ, 8, width)
        to_line(gpart, grs, S_GRAD, GRAD)
        grs[my_z] = gpart[my_z]

    first_pass(0)
    first_pass(1)
    positive_terms()
    first_pass(2)
    owner_terms(0)
    first_pass(3)
    owner_terms(1)
    for b in owner:
        invert_owner(b)
    owner_terms(2)
    second_pass(0)
    owner_terms(3)
    second_pass(1)
    second_pass(2)
    last_pass(3)

    await_line(GRAD, grs)
    grad_ref[...] = jnp.sum(grs[...], axis=0)
    await_bytes(send_sem, S_MEM, mem_ref.at[pl.ds(0, 3)])
    await_bytes(send_sem, S_LAB, labs.at[pl.ds(0, NY - 1)])
    for send, buf in ((S_IN, qall), (S_TAB, tall), (S_POS, pz), (S_GRAD, grs)):
        await_bytes(send_sem, send, buf.at[pl.ds(0, NZ - 1)])
    for c in range(NK):
        await_bytes(send_sem, S_RANK, rrs.at[c, pl.ds(0, NZ - 1)])
        await_bytes(send_sem, S_WEIGHT, wdall.at[c, pl.ds(0, NZ - 1)])


def on_device(queries, query_labels, positive_ids, positive_mask, memory, memory_labels):
    own, width = queries.shape
    rows = memory.shape[0]
    vmem = pl.BlockSpec(memory_space=pltpu.VMEM)
    smem = pl.BlockSpec(memory_space=pltpu.SMEM)
    return pl.pallas_call(
        kernel,
        out_shape=(
            jax.ShapeDtypeStruct((own,), F32),
            jax.ShapeDtypeStruct((own, width), F32),
        ),
        in_specs=[smem, vmem, vmem, vmem, vmem, pl.BlockSpec(memory_space=pltpu.HBM)],
        out_specs=(smem, vmem),
        scratch_shapes=[
            pltpu.VMEM((NY, rows, width), BF16),
            pltpu.VMEM((NY, rows // 128, 128), I32),
            pltpu.VMEM((own, 128), I32),
            pltpu.VMEM((own, 128), I16),
            pltpu.VMEM((NZ, own, width), BF16),
            pltpu.VMEM((NZ, own, 128), I16),
            pltpu.VMEM((NZ, own, 128), I32),
            pltpu.VMEM((NZ * own, rows), F32),
            pltpu.VMEM((NY * rows, 128), F32),
            pltpu.VMEM((NZ, NY * rows // 128, own, 128), I32),
            pltpu.VMEM((NY * rows, 128), F32),
            pltpu.VMEM((NZ // 2, own, 128), F32),
            pltpu.VMEM((NZ, NZ // 2, own, 128), F32),
            pltpu.VMEM((32, 128), F32),
            pltpu.VMEM((own, 64, 128), F32),
            pltpu.VMEM((24, 128), F32),
            pltpu.VMEM((2 * KB, 8, 128), F32),
            pltpu.VMEM(((NK - 1) * KB, NY * rows, 128), F32),
            pltpu.VMEM((NK, NZ, own, 128), F32),
            pltpu.VMEM((NK, NZ, own, 128), F32),
            pltpu.VMEM((own, 128), F32),
            pltpu.VMEM((NK, own, 128), F32),
            pltpu.VMEM((NK, NZ, own, 128), F32),
            pltpu.VMEM((32, 128), F32),
            pltpu.VMEM((width, NY * rows), BF16),
            pltpu.VMEM((NY * rows, 256), BF16),
            pltpu.VMEM((128, NY * rows), BF16),
            pltpu.VMEM((NZ, own, width), F32),
            pltpu.VMEM((NZ, own, width), F32),
            pltpu.SemaphoreType.DMA((N_SEND,)),
            pltpu.SemaphoreType.DMA((N_RECV,)),
            pltpu.SemaphoreType.DMA,
        ],
        compiler_params=pltpu.CompilerParams(
            collective_id=0, has_side_effects=True, vmem_limit_bytes=VMEM_LIMIT
        ),
    )(
        query_labels, queries, positive_ids, positive_mask,
        memory_labels.reshape(rows // 128, 128), memory,
    )


def solution(mesh):
    return jax.shard_map(
        on_device,
        mesh=mesh,
        in_specs=(
            P(("dp", "shard"), None),
            P(("dp", "shard")),
            P(("dp", "shard"), None),
            P(("dp", "shard"), None),
            P("shard", None),
            P("shard"),
        ),
        out_specs=(P(("dp", "shard")), P(("dp", "shard"), None)),
        check_vma=False,
    )
```

```python
import functools

import jax
import jax.numpy as jnp
from jax import lax
from jax.experimental import pallas as pl
from jax.experimental.pallas import tpu as pltpu
from jax.sharding import PartitionSpec as P

F32 = jnp.float32
BF16 = jnp.bfloat16
I32 = jnp.int32
I16 = jnp.int16
HALF_INV_TAU = 5.0
FAR = -1e6
MESH = pl.DeviceIdType.MESH
NY, NZ = 4, 8
NK, KB = 4, 8
G = 16
JC = 16
PIECES = 4
EARLY = ()
VMEM_LIMIT = 67_043_328 - 327_680
DOWN, UP, RELAY, SIB, LAB, IN, TAB, POS, RANK, WEIGHT, GRAD, N_RECV = (
    0, 4, 8, 12, 15, 16, 17, 18, 19, 23, 27, 28,
)
S_MEM, S_LAB, S_IN, S_TAB, S_POS, S_RANK, S_WEIGHT, S_GRAD, N_SEND = range(9)


def dot_nt(a, b):
    return lax.dot_general(a, b, (((1,), (1,)), ((), ())), preferred_element_type=F32)


def dot_nn(a, b):
    return lax.dot_general(a, b, (((1,), (0,)), ((), ())), preferred_element_type=F32)


def lane_gather(table, index):
    return jnp.take_along_axis(table, index, axis=1, mode="promise_in_bounds")


def twice(x):
    return jnp.transpose(jnp.concatenate([x, pltpu.roll(x, 96, axis=1)], axis=0))


def columns(x):
    return jnp.transpose(jnp.concatenate([x] * 16, axis=0))


def kernel(
    lab_ref, q_ref, id_ref, mask_ref, mlab_ref, mem_hbm, prec_ref, grad_ref,
    mem_ref, labs, tab_ref, half_ref, qall, tall, idall, s_ref, st_ref, inv_ref, ct_ref,
    ppart, pz, pt_ref, wq_ref, aux_ref,
    racc, squares, rpart, rrs, ranks, wdown, wdall, wt_ref, memt_ref, cneg_ref, cpos_ref, gpart, grs,
    send_sem, recv_sem, mem_sem,
):
    dp = lax.axis_index("dp")
    me = lax.axis_index("shard")
    block_rows, width = mem_hbm.shape
    nb = block_rows // 128
    rows = NY * block_rows
    core = lax.rem(dp, 2)
    sibling = {"dp": dp + 1 - 2 * core, "shard": me}
    my_y, my_z = lax.div(me, NZ), lax.rem(me, NZ)
    y_at = [lax.rem(my_y + d, NY) for d in range(NY)]
    z_at = [lax.rem(my_z + d, NZ) for d in range(NZ)]
    along_z = [{"shard": my_y * NZ + z_at[d]} for d in range(NZ)]
    along_y = [{"shard": y_at[d] * NZ + my_z} for d in range(NY)]
    far_first = (4, 3, 5, 2, 6, 1, 7)

    barrier = pltpu.get_barrier_semaphore()
    for peer in [along_z[d] for d in far_first] + [along_y[d] for d in (2, 1, 3)] + [sibling]:
        pl.semaphore_signal(barrier, inc=1, device_id=peer, device_id_type=MESH)

    load_memory = pltpu.make_async_copy(mem_hbm, mem_ref.at[my_y], mem_sem)
    load_memory.start()

    row = lax.broadcasted_iota(I32, (8, 64), 0)
    label = jnp.zeros((8, 64), I32)
    for i in range(8):
        label = jnp.where(row == i, lab_ref[i], label)
    tab_ref[:, 0:64] = jnp.where(mask_ref[...] > 0, id_ref[...], -1)
    tab_ref[:, 64:128] = label
    half_ref[...] = tab_ref[...].astype(I16)
    qall[my_z] = q_ref[...]
    tall[my_z] = half_ref[...]
    labs[my_y] = mlab_ref[...]

    def put(src, dst, send, recv, peer):
        pltpu.make_async_remote_copy(
            src_ref=src, dst_ref=dst, send_sem=send_sem.at[send], recv_sem=recv_sem.at[recv],
            device_id=peer, device_id_type=MESH,
        ).start()

    def await_bytes(sem, index, view):
        pltpu.make_async_copy(view, view, sem.at[index]).wait()

    def await_line(recv, buf):
        await_bytes(recv_sem, recv, buf.at[pl.ds(0, NZ - 1)])

    def to_line(src, dst, send, recv):
        for d in far_first:
            put(src.at[z_at[d]], dst.at[my_z], send, recv, along_z[d])

    def on_line(src, dst, send, recv):
        for d in far_first:
            put(src, dst.at[my_z], send, recv, along_z[d])

    def part(piece):
        return pl.ds(pl.multiple_of(core * (block_rows // 2) + piece * 128, 128), 128)

    def hand_on(block, piece, recv):
        view = mem_ref.at[block, part(piece)]
        put(view, view, S_MEM, recv, sibling)

    pl.semaphore_wait(barrier, NZ + NY - 1)
    on_line(half_ref, tall, S_TAB, TAB)
    on_line(q_ref, qall, S_IN, IN)
    for up_piece, down_piece in ((0, 2), (1, 3), (2, 0), (3, 1)):
        for piece, recv, peer in ((up_piece, DOWN, along_y[1]), (down_piece, UP, along_y[3])):
            put(mem_hbm.at[part(piece)], mem_ref.at[my_y, part(piece)], S_MEM, recv + piece, peer)
    for d in (2, 1, 3):
        put(mlab_ref, labs.at[my_y], S_LAB, LAB, along_y[d])

    def landed(block, piece, recv):
        await_bytes(recv_sem, recv + piece, mem_ref.at[block, part(piece)])

    for step in range(2):
        piece = step
        landed(y_at[3], piece, DOWN)
        view = mem_ref.at[y_at[3], part(piece)]
        put(view, view, S_MEM, RELAY + piece, along_y[1])
        hand_on(y_at[3], piece, SIB)
        piece = step + 2
        landed(y_at[1], piece, UP)
        view = mem_ref.at[y_at[1], part(piece)]
        put(view, view, S_MEM, RELAY + piece, along_y[3])
        hand_on(y_at[1], piece, SIB + 1)

    await_line(TAB, tall)
    lane = lax.broadcasted_iota(I32, (8, 128), 1)
    for i in range(NZ):
        idall[i] = tall[i].astype(I32)

    def invert(b, y):
        local = idall[b] - (y * NZ + my_z) * block_rows
        found = [jnp.full((8, 128), -1, I32) for _ in range(nb)]
        for k in range(64):
            here = jnp.broadcast_to(local[:, k : k + 1], (8, 128))
            for a in range(nb):
                found[a] = jnp.where(here == lane + a * 128, 64 + k, found[a])
        for a in range(nb):
            inv_ref[b, y * nb + a] = found[a]
        return y

    def invert_owner(b):
        def one(y, c):
            invert(b, y)
            return c

        lax.fori_loop(0, NY, one, 0)

    owner = iter(range(NZ))
    for step in range(2):
        piece = step + 2
        landed(y_at[3], piece, DOWN)
        hand_on(y_at[3], piece, SIB)
        invert_owner(next(owner))
        piece = step
        landed(y_at[1], piece, UP)
        hand_on(y_at[1], piece, SIB + 1)
        invert_owner(next(owner))
    for piece in (0, 2, 1, 3):
        landed(y_at[2], piece, RELAY)
        hand_on(y_at[2], piece, SIB + 2)
        if piece in EARLY:
            invert_owner(next(owner))

    await_line(IN, qall)
    load_memory.wait()
    queries = jnp.concatenate([qall[i].astype(F32) for i in range(NZ)], axis=0).astype(BF16)
    for step, (d, arrived) in enumerate(((0, None), (3, SIB), (1, SIB + 1), (2, SIB + 2))):
        y = y_at[d]
        if arrived is not None:
            await_bytes(recv_sem, arrived, mem_ref.at[y, pl.ds(0, block_rows // 2)])
        s_ref[...] = dot_nt(queries, mem_ref[y])
        for i in range(NZ // 2):
            pair = None
            for j in (i, i + NZ // 2):
                local = idall[j] - (y * NZ + my_z) * block_rows
                place = jnp.bitwise_and(local, 127)
                which = jnp.right_shift(local, 7)
                value = jnp.zeros((8, 128), F32)
                for a in range(nb):
                    block = s_ref[j * 8 : j * 8 + 8, a * 128 : a * 128 + 128]
                    value = jnp.where(which == a, lane_gather(block, place), value)
                value = jnp.where(lane < 64, value * HALF_INV_TAU, 0.0)
                pair = value if pair is None else pair + pltpu.roll(value, 64, axis=1)
            ppart[i] = pair if step == 0 else ppart[i] + pair
    on_line(ppart, pz, S_POS, POS)
    pz[my_z] = ppart[...]

    for _ in range(2):
        invert_owner(next(owner))
    await_bytes(recv_sem, LAB, labs.at[pl.ds(0, NY - 1)])
    queries = jnp.concatenate([queries, queries], axis=0)
    ids = idall[...].reshape(NZ * 8, 128)
    labels = jnp.transpose(jnp.concatenate([ids, ids], axis=0))[64:65, :]

    def score(y, c):
        lab_t = columns(labs[y])
        for a in range(nb):
            st = dot_nt(mem_ref[y, a * 128 : a * 128 + 128, :], queries) * HALF_INV_TAU
            column = jnp.broadcast_to(lab_t[:, a : a + 1], (128, 128))
            st_ref[pl.ds(pl.multiple_of(y * block_rows + a * 128, 128), 128), :] = jnp.where(
                column != labels, st, FAR
            )
            flipped = jnp.transpose(mem_ref[y, a * 128 : a * 128 + 128, :].astype(F32))
            memt_ref[:, pl.ds(pl.multiple_of(y * block_rows + a * 128, 128), 128)] = flipped.astype(BF16)
        return c

    lax.fori_loop(0, NY, score, 0)

    await_line(POS, pz)
    pos = jnp.sum(pz[...], axis=0)
    half_line = NZ // 2
    own = jnp.where(lane < 64, pos[0], 0.0)
    for i in range(1, NZ):
        block = pos[i % half_line]
        block = pltpu.roll(block, 64, axis=1) if i >= half_line else block
        own = jnp.where(jnp.logical_and(my_z == i, lane < 64), block, own)
    pos = pos.reshape(half_line * 8, 128)
    pt_ref[...] = twice(jnp.concatenate([pos, pltpu.roll(pos, 64, axis=1)], axis=0))[:32, :]
    zero = jnp.zeros((8, 128), F32)
    mask = jnp.where(jnp.logical_and(lane < 64, tab_ref[...] >= 0), 1.0, 0.0)
    found = jnp.sum(mask, axis=1, keepdims=True)

    def first_pass(c):
        p = [jnp.broadcast_to(pt_ref[c * KB + i : c * KB + i + 1, :], (8, 128)) for i in range(KB)]

        def step(g, acc):
            acc = list(acc)
            at = [pl.ds(pl.multiple_of(g * (8 * G), 8 * G) + 8 * v, 8) for v in range(G)]
            for i in range(KB):
                one = two = None
                for v in range(G):
                    t = jnp.tanh(st_ref[at[v], :] - p[i])
                    tt = t * t
                    if c:
                        squares[(c - 1) * KB + i, at[v], :] = tt
                    one = t if one is None else one + t
                    two = tt if two is None else two + tt
                acc[2 * i] = acc[2 * i] + (one + float(G))
                acc[2 * i + 1] = acc[2 * i + 1] + (float(G) - two)
            return tuple(acc)

        acc = lax.fori_loop(0, rows // (8 * G), step, (zero,) * (2 * KB), unroll=4)
        for i in range(KB):
            racc[i] = acc[2 * i]
            racc[KB + i] = acc[2 * i + 1]
        sums = jnp.sum(racc[...], axis=1)
        spread = [jnp.zeros((8, 128), F32)] * 16
        spread[c] = 0.5 * sums[:KB, :]
        spread[8 + c] = 0.25 * sums[KB:, :]
        both = jnp.transpose(jnp.concatenate(spread, axis=0))
        both = both[:64, :] + pltpu.roll(both[64:, :], 32, axis=1)
        rpart[c] = both.reshape(NZ, 8, 128)
        to_line(rpart.at[c], rrs.at[c], S_RANK, RANK + c)
        rrs[c, my_z] = rpart[c, my_z]

    def positive_terms():
        own_t = columns(own)
        mask_t = columns(mask)
        off = jnp.where(
            lax.broadcasted_iota(I32, (64, 128), 0) == lax.broadcasted_iota(I32, (64, 128), 1),
            0.0, 1.0,
        )
        for i in range(8):
            col = jnp.broadcast_to(own_t[:64, i : i + 1], (64, 128))
            mcol = jnp.broadcast_to(mask_t[:64, i : i + 1], (64, 128)) * off
            t = jnp.tanh(col - own[i : i + 1, :])
            w = (1.0 - t * t) * (0.25 * off)
            wq_ref[i] = w
            aux_ref[i : i + 1, :] = 1.0 + jnp.sum(mcol * (0.5 + 0.5 * t), axis=0, keepdims=True)
            aux_ref[8 + i : 9 + i, :] = jnp.sum(mcol * w, axis=0, keepdims=True)

    def owner_terms(c):
        await_line(RANK + c, rrs.at[c])
        rank_neg = jnp.sum(rrs[c], axis=0)
        if c:
            rank_neg = rank_neg + ranks[...]
        ranks[...] = rank_neg
        rank_pos = aux_ref[0:8, :]
        total = rank_pos + rank_neg
        share = mask / (found * total * total)
        weight_neg = share * rank_pos
        both = jnp.where(lane < 64, weight_neg * (0.5 * HALF_INV_TAU), 0.0)
        if c == NK - 1:
            slope_neg = pltpu.roll(rank_neg, 64, axis=1)
            spread = aux_ref[8:16, :]
            weight_pos = -share * rank_neg
            wp_t = columns(weight_pos)
            for i in range(8):
                col = jnp.broadcast_to(wp_t[:64, i : i + 1], (64, 128))
                aux_ref[16 + i : 17 + i, :] = jnp.sum(col * wq_ref[i], axis=0, keepdims=True)
            backed = aux_ref[16:24, :]
            dpos = mask * backed - weight_neg * slope_neg - weight_pos * spread
            dpos = pltpu.roll(dpos * (2.0 * HALF_INV_TAU), 64, axis=1)
            both = jnp.where(lane < 64, both, dpos)
        wdown[c] = both
        on_line(wdown.at[c], wdall.at[c], S_WEIGHT, WEIGHT + c)
        wdall[c, my_z] = both
        if c == NK - 1:
            precision = jnp.sum(mask * rank_pos / total, axis=1, keepdims=True) / found
            for i in range(8):
                prec_ref[i] = precision[i, 0]

    def weigh(c, at, acc):
        for i in range(KB):
            w = jnp.broadcast_to(wt_ref[c * KB + i : c * KB + i + 1, :], (8, 128))
            if not c:
                p = jnp.broadcast_to(pt_ref[i : i + 1, :], (8, 128))
            for v in range(len(at)):
                if c:
                    tt = squares[(c - 1) * KB + i, at[v], :]
                else:
                    t = jnp.tanh(st_ref[at[v], :] - p)
                    tt = t * t
                acc[v] = acc[v] + w * (1.0 - tt)
        return acc

    def await_weights(c):
        await_line(WEIGHT + c, wdall.at[c])
        weights = twice(wdall[c].reshape(NZ * 8, 128))
        wt_ref[c * KB : c * KB + KB, :] = weights[c * KB : c * KB + KB, :]

    def second_pass(c):
        await_weights(c)

        def block(jb, carry):
            start = pl.multiple_of(jb * (8 * JC), 8 * JC)
            at = [pl.ds(start + 8 * v, 8) for v in range(JC)]
            acc = weigh(c, at, [ct_ref[at[v], :] if c else zero for v in range(JC)])
            for v in range(JC):
                ct_ref[at[v], :] = acc[v]
            return carry

        lax.fori_loop(0, rows // (8 * JC), block, 0, unroll=2)

    def last_pass(c):
        await_weights(c)
        def block(a, carry):
            start = pl.multiple_of(a * 128, 128)
            at = [pl.ds(start + 8 * v, 8) for v in range(16)]
            acc = weigh(c, at, [ct_ref[at[v], :] for v in range(16)])
            neg = jnp.concatenate(acc, axis=0)
            top = neg.astype(BF16)
            cneg_ref[pl.ds(start, 128), 0:128] = top
            cneg_ref[pl.ds(start, 128), 128:256] = (neg - top.astype(F32)).astype(BF16)
            pos = []
            for i in range(NZ):
                index = inv_ref[i, a]
                value = lane_gather(wdall[c, i], jnp.bitwise_and(index, 127))
                pos.append(jnp.where(index >= 0, value, 0.0))
            pos = jnp.concatenate(pos, axis=0)
            top = pos.astype(BF16)
            cpos_ref[0:64, pl.ds(start, 128)] = top
            cpos_ref[64:128, pl.ds(start, 128)] = (pos - top.astype(F32)).astype(BF16)
            return carry

        lax.fori_loop(0, rows // 128, block, 0, unroll=4)
        neg = pos = None
        for y in range(NY):
            span = slice(y * block_rows, (y + 1) * block_rows)
            one = dot_nn(memt_ref[:, span], cneg_ref[span, :])
            two = dot_nn(cpos_ref[:, span], mem_ref[y])
            neg = one if neg is None else neg + one
            pos = two if pos is None else pos + two
        neg = jnp.transpose(neg[:, :128] + neg[:, 128:])
        grad = neg[:64, :] + neg[64:, :] + pos[:64, :] + pos[64:, :]
        gpart[...] = grad.reshape(NZ, 8, width)
        to_line(gpart, grs, S_GRAD, GRAD)
        grs[my_z] = gpart[my_z]

    first_pass(0)
    first_pass(1)
    positive_terms()
    first_pass(2)
    owner_terms(0)
    first_pass(3)
    owner_terms(1)
    for b in owner:
        invert_owner(b)
    owner_terms(2)
    second_pass(0)
    owner_terms(3)
    second_pass(1)
    second_pass(2)
    last_pass(3)

    await_line(GRAD, grs)
    grad_ref[...] = jnp.sum(grs[...], axis=0)
    await_bytes(send_sem, S_MEM, mem_ref.at[pl.ds(0, 3)])
    await_bytes(send_sem, S_LAB, labs.at[pl.ds(0, NY - 1)])
    for send, buf in ((S_IN, qall), (S_TAB, tall), (S_POS, pz), (S_GRAD, grs)):
        await_bytes(send_sem, send, buf.at[pl.ds(0, NZ - 1)])
    for c in range(NK):
        await_bytes(send_sem, S_RANK, rrs.at[c, pl.ds(0, NZ - 1)])
        await_bytes(send_sem, S_WEIGHT, wdall.at[c, pl.ds(0, NZ - 1)])


def hand_over(prec_in, grad_in, prec_out, grad_out):
    for i in range(8):
        prec_out[i] = prec_in[i]
    grad_out[...] = grad_in[...]


def on_device(queries, query_labels, positive_ids, positive_mask, memory, memory_labels):
    own, width = queries.shape
    rows = memory.shape[0]
    vmem = pl.BlockSpec(memory_space=pltpu.VMEM)
    smem = pl.BlockSpec(memory_space=pltpu.SMEM)
    precision, grad = pl.pallas_call(
        kernel,
        out_shape=(
            jax.ShapeDtypeStruct((own,), F32),
            jax.ShapeDtypeStruct((own, width), F32),
        ),
        in_specs=[smem, vmem, vmem, vmem, vmem, pl.BlockSpec(memory_space=pltpu.HBM)],
        out_specs=(smem, vmem),
        scratch_shapes=[
            pltpu.VMEM((NY, rows, width), BF16),
            pltpu.VMEM((NY, rows // 128, 128), I32),
            pltpu.VMEM((own, 128), I32),
            pltpu.VMEM((own, 128), I16),
            pltpu.VMEM((NZ, own, width), BF16),
            pltpu.VMEM((NZ, own, 128), I16),
            pltpu.VMEM((NZ, own, 128), I32),
            pltpu.VMEM((NZ * own, rows), F32),
            pltpu.VMEM((NY * rows, 128), F32),
            pltpu.VMEM((NZ, NY * rows // 128, own, 128), I32),
            pltpu.VMEM((NY * rows, 128), F32),
            pltpu.VMEM((NZ // 2, own, 128), F32),
            pltpu.VMEM((NZ, NZ // 2, own, 128), F32),
            pltpu.VMEM((32, 128), F32),
            pltpu.VMEM((own, 64, 128), F32),
            pltpu.VMEM((24, 128), F32),
            pltpu.VMEM((2 * KB, 8, 128), F32),
            pltpu.VMEM(((NK - 1) * KB, NY * rows, 128), F32),
            pltpu.VMEM((NK, NZ, own, 128), F32),
            pltpu.VMEM((NK, NZ, own, 128), F32),
            pltpu.VMEM((own, 128), F32),
            pltpu.VMEM((NK, own, 128), F32),
            pltpu.VMEM((NK, NZ, own, 128), F32),
            pltpu.VMEM((32, 128), F32),
            pltpu.VMEM((width, NY * rows), BF16),
            pltpu.VMEM((NY * rows, 256), BF16),
            pltpu.VMEM((128, NY * rows), BF16),
            pltpu.VMEM((NZ, own, width), F32),
            pltpu.VMEM((NZ, own, width), F32),
            pltpu.SemaphoreType.DMA((N_SEND,)),
            pltpu.SemaphoreType.DMA((N_RECV,)),
            pltpu.SemaphoreType.DMA,
        ],
        compiler_params=pltpu.CompilerParams(
            collective_id=0, has_side_effects=True, vmem_limit_bytes=VMEM_LIMIT
        ),
    )(
        query_labels, queries, positive_ids, positive_mask,
        memory_labels.reshape(rows // 128, 128), memory,
    )
    return pl.pallas_call(
        hand_over,
        out_shape=(
            jax.ShapeDtypeStruct((own,), F32),
            jax.ShapeDtypeStruct((own, width), F32),
        ),
        in_specs=[smem, vmem],
        out_specs=(smem, vmem),
    )(precision, grad)


def solution(mesh):
    return jax.shard_map(
        on_device,
        mesh=mesh,
        in_specs=(
            P(("dp", "shard"), None),
            P(("dp", "shard")),
            P(("dp", "shard"), None),
            P(("dp", "shard"), None),
            P("shard", None),
            P("shard"),
        ),
        out_specs=(P(("dp", "shard")), P(("dp", "shard"), None)),
        check_vma=False,
    )
```

```python
import functools

import jax
import jax.numpy as jnp
from jax import lax
from jax.experimental import pallas as pl
from jax.experimental.pallas import tpu as pltpu
from jax.sharding import PartitionSpec as P

F32 = jnp.float32
BF16 = jnp.bfloat16
I32 = jnp.int32
I16 = jnp.int16
HALF_INV_TAU = 5.0
FAR = -1e6
MESH = pl.DeviceIdType.MESH
NY, NZ = 4, 8
NK, KB = 4, 8
G = 16
JC = 16
PIECES = 4
EARLY = ()
VMEM_LIMIT = 67_043_328 - 327_680
DOWN, UP, RELAY, SIB, LAB, IN, TAB, POS, RANK, WEIGHT, GRAD, N_RECV = (
    0, 4, 8, 12, 15, 16, 17, 18, 19, 23, 27, 28,
)
S_MEM, S_LAB, S_IN, S_TAB, S_POS, S_RANK, S_WEIGHT, S_GRAD, N_SEND = range(9)


def dot_nt(a, b):
    return lax.dot_general(a, b, (((1,), (1,)), ((), ())), preferred_element_type=F32)


def dot_nn(a, b):
    return lax.dot_general(a, b, (((1,), (0,)), ((), ())), preferred_element_type=F32)


def lane_gather(table, index):
    return jnp.take_along_axis(table, index, axis=1, mode="promise_in_bounds")


def twice(x):
    return jnp.transpose(jnp.concatenate([x, pltpu.roll(x, 96, axis=1)], axis=0))


def columns(x):
    return jnp.transpose(jnp.concatenate([x] * 16, axis=0))


def kernel(
    lab_ref, q_ref, id_ref, mask_ref, mlab_ref, mem_hbm, prec_ref, grad_ref,
    mem_ref, labs, tab_ref, half_ref, qall, tall, idall, s_ref, st_ref, inv_ref, ct_ref,
    ppart, pz, pt_ref, wq_ref, aux_ref,
    racc, squares, rpart, rrs, ranks, wdown, wdall, wt_ref, memt_ref, cneg_ref, cpos_ref, gpart, grs,
    send_sem, recv_sem, mem_sem,
):
    dp = lax.axis_index("dp")
    me = lax.axis_index("shard")
    block_rows, width = mem_hbm.shape
    nb = block_rows // 128
    rows = NY * block_rows
    core = lax.rem(dp, 2)
    sibling = {"dp": dp + 1 - 2 * core, "shard": me}
    my_y, my_z = lax.div(me, NZ), lax.rem(me, NZ)
    y_at = [lax.rem(my_y + d, NY) for d in range(NY)]
    z_at = [lax.rem(my_z + d, NZ) for d in range(NZ)]
    along_z = [{"shard": my_y * NZ + z_at[d]} for d in range(NZ)]
    along_y = [{"shard": y_at[d] * NZ + my_z} for d in range(NY)]
    far_first = (4, 3, 5, 2, 6, 1, 7)

    barrier = pltpu.get_barrier_semaphore()
    for peer in [along_z[d] for d in far_first] + [along_y[d] for d in (2, 1, 3)] + [sibling]:
        pl.semaphore_signal(barrier, inc=1, device_id=peer, device_id_type=MESH)

    load_memory = pltpu.make_async_copy(mem_hbm, mem_ref.at[my_y], mem_sem)
    load_memory.start()

    row = lax.broadcasted_iota(I32, (8, 64), 0)
    label = jnp.zeros((8, 64), I32)
    for i in range(8):
        label = jnp.where(row == i, lab_ref[i], label)
    tab_ref[:, 0:64] = jnp.where(mask_ref[...] > 0, id_ref[...], -1)
    tab_ref[:, 64:128] = label
    half_ref[...] = tab_ref[...].astype(I16)
    qall[my_z] = q_ref[...]
    tall[my_z] = half_ref[...]
    labs[my_y] = mlab_ref[...]

    def put(src, dst, send, recv, peer):
        pltpu.make_async_remote_copy(
            src_ref=src, dst_ref=dst, send_sem=send_sem.at[send], recv_sem=recv_sem.at[recv],
            device_id=peer, device_id_type=MESH,
        ).start()

    def await_bytes(sem, index, view):
        pltpu.make_async_copy(view, view, sem.at[index]).wait()

    def await_line(recv, buf):
        await_bytes(recv_sem, recv, buf.at[pl.ds(0, NZ - 1)])

    def to_line(src, dst, send, recv):
        for d in far_first:
            put(src.at[z_at[d]], dst.at[my_z], send, recv, along_z[d])

    def on_line(src, dst, send, recv):
        for d in far_first:
            put(src, dst.at[my_z], send, recv, along_z[d])

    def part(piece):
        return pl.ds(pl.multiple_of(core * (block_rows // 2) + piece * 128, 128), 128)

    def hand_on(block, piece, recv):
        view = mem_ref.at[block, part(piece)]
        put(view, view, S_MEM, recv, sibling)

    pl.semaphore_wait(barrier, NZ + NY - 1)
    on_line(half_ref, tall, S_TAB, TAB)
    on_line(q_ref, qall, S_IN, IN)
    for up_piece, down_piece in ((0, 2), (1, 3), (2, 0), (3, 1)):
        for piece, recv, peer in ((up_piece, DOWN, along_y[1]), (down_piece, UP, along_y[3])):
            put(mem_hbm.at[part(piece)], mem_ref.at[my_y, part(piece)], S_MEM, recv + piece, peer)
    for d in (2, 1, 3):
        put(mlab_ref, labs.at[my_y], S_LAB, LAB, along_y[d])

    def landed(block, piece, recv):
        await_bytes(recv_sem, recv + piece, mem_ref.at[block, part(piece)])

    for step in range(2):
        piece = step
        landed(y_at[3], piece, DOWN)
        view = mem_ref.at[y_at[3], part(piece)]
        put(view, view, S_MEM, RELAY + piece, along_y[1])
        hand_on(y_at[3], piece, SIB)
        piece = step + 2
        landed(y_at[1], piece, UP)
        view = mem_ref.at[y_at[1], part(piece)]
        put(view, view, S_MEM, RELAY + piece, along_y[3])
        hand_on(y_at[1], piece, SIB + 1)

    await_line(TAB, tall)
    lane = lax.broadcasted_iota(I32, (8, 128), 1)
    for i in range(NZ):
        idall[i] = tall[i].astype(I32)

    def invert(b, y):
        local = idall[b] - (y * NZ + my_z) * block_rows
        found = [jnp.full((8, 128), -1, I32) for _ in range(nb)]
        for k in range(64):
            here = jnp.broadcast_to(local[:, k : k + 1], (8, 128))
            for a in range(nb):
                found[a] = jnp.where(here == lane + a * 128, 64 + k, found[a])
        for a in range(nb):
            inv_ref[b, y * nb + a] = found[a]
        return y

    def invert_owner(b):
        def one(y, c):
            invert(b, y)
            return c

        lax.fori_loop(0, NY, one, 0)

    owner = iter(range(NZ))
    for step in range(2):
        piece = step + 2
        landed(y_at[3], piece, DOWN)
        hand_on(y_at[3], piece, SIB)
        invert_owner(next(owner))
        piece = step
        landed(y_at[1], piece, UP)
        hand_on(y_at[1], piece, SIB + 1)
        invert_owner(next(owner))
    for piece in (0, 2, 1, 3):
        landed(y_at[2], piece, RELAY)
        hand_on(y_at[2], piece, SIB + 2)
        if piece in EARLY:
            invert_owner(next(owner))

    await_line(IN, qall)
    load_memory.wait()
    queries = jnp.concatenate([qall[i].astype(F32) for i in range(NZ)], axis=0).astype(BF16)
    for step, (d, arrived) in enumerate(((0, None), (3, SIB), (1, SIB + 1), (2, SIB + 2))):
        y = y_at[d]
        if arrived is not None:
            await_bytes(recv_sem, arrived, mem_ref.at[y, pl.ds(0, block_rows // 2)])
        s_ref[...] = dot_nt(queries, mem_ref[y])
        for i in range(NZ // 2):
            pair = None
            for j in (i, i + NZ // 2):
                local = idall[j] - (y * NZ + my_z) * block_rows
                place = jnp.bitwise_and(local, 127)
                which = jnp.right_shift(local, 7)
                value = jnp.zeros((8, 128), F32)
                for a in range(nb):
                    block = s_ref[j * 8 : j * 8 + 8, a * 128 : a * 128 + 128]
                    value = jnp.where(which == a, lane_gather(block, place), value)
                value = jnp.where(lane < 64, value * HALF_INV_TAU, 0.0)
                pair = value if pair is None else pair + pltpu.roll(value, 64, axis=1)
            ppart[i] = pair if step == 0 else ppart[i] + pair
    on_line(ppart, pz, S_POS, POS)
    pz[my_z] = ppart[...]

    for _ in range(3):
        invert_owner(next(owner))
    await_bytes(recv_sem, LAB, labs.at[pl.ds(0, NY - 1)])
    queries = jnp.concatenate([queries, queries], axis=0)
    ids = idall[...].reshape(NZ * 8, 128)
    labels = jnp.transpose(jnp.concatenate([ids, ids], axis=0))[64:65, :]

    def score(y, c):
        lab_t = columns(labs[y])
        for a in range(nb):
            st = dot_nt(mem_ref[y, a * 128 : a * 128 + 128, :], queries) * HALF_INV_TAU
            column = jnp.broadcast_to(lab_t[:, a : a + 1], (128, 128))
            st_ref[pl.ds(pl.multiple_of(y * block_rows + a * 128, 128), 128), :] = jnp.where(
                column != labels, st, FAR
            )
            flipped = jnp.transpose(mem_ref[y, a * 128 : a * 128 + 128, :].astype(F32))
            memt_ref[:, pl.ds(pl.multiple_of(y * block_rows + a * 128, 128), 128)] = flipped.astype(BF16)
        return c

    lax.fori_loop(0, NY, score, 0)

    await_line(POS, pz)
    pos = jnp.sum(pz[...], axis=0)
    half_line = NZ // 2
    own = jnp.where(lane < 64, pos[0], 0.0)
    for i in range(1, NZ):
        block = pos[i % half_line]
        block = pltpu.roll(block, 64, axis=1) if i >= half_line else block
        own = jnp.where(jnp.logical_and(my_z == i, lane < 64), block, own)
    pos = pos.reshape(half_line * 8, 128)
    pt_ref[...] = twice(jnp.concatenate([pos, pltpu.roll(pos, 64, axis=1)], axis=0))[:32, :]
    zero = jnp.zeros((8, 128), F32)
    mask = jnp.where(jnp.logical_and(lane < 64, tab_ref[...] >= 0), 1.0, 0.0)
    found = jnp.sum(mask, axis=1, keepdims=True)

    def first_pass(c):
        p = [jnp.broadcast_to(pt_ref[c * KB + i : c * KB + i + 1, :], (8, 128)) for i in range(KB)]

        def step(g, acc):
            acc = list(acc)
            at = [pl.ds(pl.multiple_of(g * (8 * G), 8 * G) + 8 * v, 8) for v in range(G)]
            for i in range(KB):
                one = two = None
                for v in range(G):
                    t = jnp.tanh(st_ref[at[v], :] - p[i])
                    tt = t * t
                    if c:
                        squares[(c - 1) * KB + i, at[v], :] = tt
                    one = t if one is None else one + t
                    two = tt if two is None else two + tt
                acc[2 * i] = acc[2 * i] + (one + float(G))
                acc[2 * i + 1] = acc[2 * i + 1] + (float(G) - two)
            return tuple(acc)

        acc = lax.fori_loop(0, rows // (8 * G), step, (zero,) * (2 * KB), unroll=4)
        for i in range(KB):
            racc[i] = acc[2 * i]
            racc[KB + i] = acc[2 * i + 1]
        sums = jnp.sum(racc[...], axis=1)
        spread = [jnp.zeros((8, 128), F32)] * 16
        spread[c] = 0.5 * sums[:KB, :]
        spread[8 + c] = 0.25 * sums[KB:, :]
        both = jnp.transpose(jnp.concatenate(spread, axis=0))
        both = both[:64, :] + pltpu.roll(both[64:, :], 32, axis=1)
        rpart[c] = both.reshape(NZ, 8, 128)
        to_line(rpart.at[c], rrs.at[c], S_RANK, RANK + c)
        rrs[c, my_z] = rpart[c, my_z]

    def positive_terms():
        own_t = columns(own)
        mask_t = columns(mask)
        off = jnp.where(
            lax.broadcasted_iota(I32, (64, 128), 0) == lax.broadcasted_iota(I32, (64, 128), 1),
            0.0, 1.0,
        )
        for i in range(8):
            col = jnp.broadcast_to(own_t[:64, i : i + 1], (64, 128))
            mcol = jnp.broadcast_to(mask_t[:64, i : i + 1], (64, 128)) * off
            t = jnp.tanh(col - own[i : i + 1, :])
            w = (1.0 - t * t) * (0.25 * off)
            wq_ref[i] = w
            aux_ref[i : i + 1, :] = 1.0 + jnp.sum(mcol * (0.5 + 0.5 * t), axis=0, keepdims=True)
            aux_ref[8 + i : 9 + i, :] = jnp.sum(mcol * w, axis=0, keepdims=True)

    def owner_terms(c):
        await_line(RANK + c, rrs.at[c])
        rank_neg = jnp.sum(rrs[c], axis=0)
        if c:
            rank_neg = rank_neg + ranks[...]
        ranks[...] = rank_neg
        rank_pos = aux_ref[0:8, :]
        total = rank_pos + rank_neg
        share = mask / (found * total * total)
        weight_neg = share * rank_pos
        both = jnp.where(lane < 64, weight_neg * (0.5 * HALF_INV_TAU), 0.0)
        if c == NK - 1:
            slope_neg = pltpu.roll(rank_neg, 64, axis=1)
            spread = aux_ref[8:16, :]
            weight_pos = -share * rank_neg
            wp_t = columns(weight_pos)
            for i in range(8):
                col = jnp.broadcast_to(wp_t[:64, i : i + 1], (64, 128))
                aux_ref[16 + i : 17 + i, :] = jnp.sum(col * wq_ref[i], axis=0, keepdims=True)
            backed = aux_ref[16:24, :]
            dpos = mask * backed - weight_neg * slope_neg - weight_pos * spread
            dpos = pltpu.roll(dpos * (2.0 * HALF_INV_TAU), 64, axis=1)
            both = jnp.where(lane < 64, both, dpos)
        wdown[c] = both
        on_line(wdown.at[c], wdall.at[c], S_WEIGHT, WEIGHT + c)
        wdall[c, my_z] = both
        if c == NK - 1:
            precision = jnp.sum(mask * rank_pos / total, axis=1, keepdims=True) / found
            for i in range(8):
                prec_ref[i] = precision[i, 0]

    def weigh(c, at, acc):
        for i in range(KB):
            w = jnp.broadcast_to(wt_ref[c * KB + i : c * KB + i + 1, :], (8, 128))
            if not c:
                p = jnp.broadcast_to(pt_ref[i : i + 1, :], (8, 128))
            for v in range(len(at)):
                if c:
                    tt = squares[(c - 1) * KB + i, at[v], :]
                else:
                    t = jnp.tanh(st_ref[at[v], :] - p)
                    tt = t * t
                acc[v] = acc[v] + w * (1.0 - tt)
        return acc

    def await_weights(c):
        await_line(WEIGHT + c, wdall.at[c])
        weights = twice(wdall[c].reshape(NZ * 8, 128))
        wt_ref[c * KB : c * KB + KB, :] = weights[c * KB : c * KB + KB, :]

    def second_pass(c):
        await_weights(c)

        def block(jb, carry):
            start = pl.multiple_of(jb * (8 * JC), 8 * JC)
            at = [pl.ds(start + 8 * v, 8) for v in range(JC)]
            acc = weigh(c, at, [ct_ref[at[v], :] if c else zero for v in range(JC)])
            for v in range(JC):
                ct_ref[at[v], :] = acc[v]
            return carry

        lax.fori_loop(0, rows // (8 * JC), block, 0, unroll=2)

    def last_pass(c):
        await_weights(c)
        def block(a, carry):
            start = pl.multiple_of(a * 128, 128)
            at = [pl.ds(start + 8 * v, 8) for v in range(16)]
            acc = weigh(c, at, [ct_ref[at[v], :] for v in range(16)])
            neg = jnp.concatenate(acc, axis=0)
            top = neg.astype(BF16)
            cneg_ref[pl.ds(start, 128), 0:128] = top
            cneg_ref[pl.ds(start, 128), 128:256] = (neg - top.astype(F32)).astype(BF16)
            pos = []
            for i in range(NZ):
                index = inv_ref[i, a]
                value = lane_gather(wdall[c, i], jnp.bitwise_and(index, 127))
                pos.append(jnp.where(index >= 0, value, 0.0))
            pos = jnp.concatenate(pos, axis=0)
            top = pos.astype(BF16)
            cpos_ref[0:64, pl.ds(start, 128)] = top
            cpos_ref[64:128, pl.ds(start, 128)] = (pos - top.astype(F32)).astype(BF16)
            return carry

        lax.fori_loop(0, rows // 128, block, 0, unroll=4)
        neg = pos = None
        for y in range(NY):
            span = slice(y * block_rows, (y + 1) * block_rows)
            one = dot_nn(memt_ref[:, span], cneg_ref[span, :])
            two = dot_nn(cpos_ref[:, span], mem_ref[y])
            neg = one if neg is None else neg + one
            pos = two if pos is None else pos + two
        neg = jnp.transpose(neg[:, :128] + neg[:, 128:])
        grad = neg[:64, :] + neg[64:, :] + pos[:64, :] + pos[64:, :]
        gpart[...] = grad.reshape(NZ, 8, width)
        to_line(gpart, grs, S_GRAD, GRAD)
        grs[my_z] = gpart[my_z]

    first_pass(0)
    first_pass(1)
    positive_terms()
    first_pass(2)
    owner_terms(0)
    first_pass(3)
    owner_terms(1)
    for b in owner:
        invert_owner(b)
    owner_terms(2)
    second_pass(0)
    owner_terms(3)
    second_pass(1)
    second_pass(2)
    last_pass(3)

    await_line(GRAD, grs)
    grad_ref[...] = jnp.sum(grs[...], axis=0)
    await_bytes(send_sem, S_MEM, mem_ref.at[pl.ds(0, 3)])
    await_bytes(send_sem, S_LAB, labs.at[pl.ds(0, NY - 1)])
    for send, buf in ((S_IN, qall), (S_TAB, tall), (S_POS, pz), (S_GRAD, grs)):
        await_bytes(send_sem, send, buf.at[pl.ds(0, NZ - 1)])
    for c in range(NK):
        await_bytes(send_sem, S_RANK, rrs.at[c, pl.ds(0, NZ - 1)])
        await_bytes(send_sem, S_WEIGHT, wdall.at[c, pl.ds(0, NZ - 1)])


def hand_over(prec_in, grad_in, prec_out, grad_out):
    for i in range(8):
        prec_out[i] = prec_in[i]
    grad_out[...] = grad_in[...]


def on_device(queries, query_labels, positive_ids, positive_mask, memory, memory_labels):
    own, width = queries.shape
    rows = memory.shape[0]
    vmem = pl.BlockSpec(memory_space=pltpu.VMEM)
    smem = pl.BlockSpec(memory_space=pltpu.SMEM)
    precision, grad = pl.pallas_call(
        kernel,
        out_shape=(
            jax.ShapeDtypeStruct((own,), F32),
            jax.ShapeDtypeStruct((own, width), F32),
        ),
        in_specs=[smem, vmem, vmem, vmem, vmem, pl.BlockSpec(memory_space=pltpu.HBM)],
        out_specs=(smem, vmem),
        scratch_shapes=[
            pltpu.VMEM((NY, rows, width), BF16),
            pltpu.VMEM((NY, rows // 128, 128), I32),
            pltpu.VMEM((own, 128), I32),
            pltpu.VMEM((own, 128), I16),
            pltpu.VMEM((NZ, own, width), BF16),
            pltpu.VMEM((NZ, own, 128), I16),
            pltpu.VMEM((NZ, own, 128), I32),
            pltpu.VMEM((NZ * own, rows), F32),
            pltpu.VMEM((NY * rows, 128), F32),
            pltpu.VMEM((NZ, NY * rows // 128, own, 128), I32),
            pltpu.VMEM((NY * rows, 128), F32),
            pltpu.VMEM((NZ // 2, own, 128), F32),
            pltpu.VMEM((NZ, NZ // 2, own, 128), F32),
            pltpu.VMEM((32, 128), F32),
            pltpu.VMEM((own, 64, 128), F32),
            pltpu.VMEM((24, 128), F32),
            pltpu.VMEM((2 * KB, 8, 128), F32),
            pltpu.VMEM(((NK - 1) * KB, NY * rows, 128), F32),
            pltpu.VMEM((NK, NZ, own, 128), F32),
            pltpu.VMEM((NK, NZ, own, 128), F32),
            pltpu.VMEM((own, 128), F32),
            pltpu.VMEM((NK, own, 128), F32),
            pltpu.VMEM((NK, NZ, own, 128), F32),
            pltpu.VMEM((32, 128), F32),
            pltpu.VMEM((width, NY * rows), BF16),
            pltpu.VMEM((NY * rows, 256), BF16),
            pltpu.VMEM((128, NY * rows), BF16),
            pltpu.VMEM((NZ, own, width), F32),
            pltpu.VMEM((NZ, own, width), F32),
            pltpu.SemaphoreType.DMA((N_SEND,)),
            pltpu.SemaphoreType.DMA((N_RECV,)),
            pltpu.SemaphoreType.DMA,
        ],
        compiler_params=pltpu.CompilerParams(
            collective_id=0, has_side_effects=True, vmem_limit_bytes=VMEM_LIMIT
        ),
    )(
        query_labels, queries, positive_ids, positive_mask,
        memory_labels.reshape(rows // 128, 128), memory,
    )
    return pl.pallas_call(
        hand_over,
        out_shape=(
            jax.ShapeDtypeStruct((own,), F32),
            jax.ShapeDtypeStruct((own, width), F32),
        ),
        in_specs=[smem, vmem],
        out_specs=(smem, vmem),
    )(precision, grad)


def solution(mesh):
    return jax.shard_map(
        on_device,
        mesh=mesh,
        in_specs=(
            P(("dp", "shard"), None),
            P(("dp", "shard")),
            P(("dp", "shard"), None),
            P(("dp", "shard"), None),
            P("shard", None),
            P("shard"),
        ),
        out_specs=(P(("dp", "shard")), P(("dp", "shard"), None)),
        check_vma=False,
    )
```

```python
import functools

import jax
import jax.numpy as jnp
from jax import lax
from jax.experimental import pallas as pl
from jax.experimental.pallas import tpu as pltpu
from jax.sharding import PartitionSpec as P

F32 = jnp.float32
BF16 = jnp.bfloat16
I32 = jnp.int32
I16 = jnp.int16
HALF_INV_TAU = 5.0
FAR = -1e6
MESH = pl.DeviceIdType.MESH
NY, NZ = 4, 8
NK, KB = 4, 8
G = 16
JC = 16
PIECES = 4
EARLY = ()
VMEM_LIMIT = 67_043_328 - 327_680
DOWN, UP, RELAY, SIB, LAB, IN, TAB, POS, RANK, WEIGHT, GRAD, N_RECV = (
    0, 4, 8, 12, 15, 16, 17, 18, 19, 23, 27, 28,
)
S_MEM, S_LAB, S_IN, S_TAB, S_POS, S_RANK, S_WEIGHT, S_GRAD, N_SEND = range(9)


def dot_nt(a, b):
    return lax.dot_general(a, b, (((1,), (1,)), ((), ())), preferred_element_type=F32)


def dot_nn(a, b):
    return lax.dot_general(a, b, (((1,), (0,)), ((), ())), preferred_element_type=F32)


def lane_gather(table, index):
    return jnp.take_along_axis(table, index, axis=1, mode="promise_in_bounds")


def twice(x):
    return jnp.transpose(jnp.concatenate([x, pltpu.roll(x, 96, axis=1)], axis=0))


def columns(x):
    return jnp.transpose(jnp.concatenate([x] * 16, axis=0))


def kernel(
    lab_ref, q_ref, id_ref, mask_ref, mlab_ref, mem_hbm, prec_ref, grad_ref,
    mem_ref, labs, tab_ref, half_ref, qall, tall, idall, s_ref, st_ref, inv_ref, ct_ref,
    ppart, pz, pt_ref, wq_ref, aux_ref,
    racc, squares, rpart, rrs, ranks, wdown, wdall, wt_ref, memt_ref, cneg_ref, cpos_ref, gpart, grs,
    send_sem, recv_sem, mem_sem,
):
    dp = lax.axis_index("dp")
    me = lax.axis_index("shard")
    block_rows, width = mem_hbm.shape
    nb = block_rows // 128
    rows = NY * block_rows
    core = lax.rem(dp, 2)
    sibling = {"dp": dp + 1 - 2 * core, "shard": me}
    my_y, my_z = lax.div(me, NZ), lax.rem(me, NZ)
    y_at = [lax.rem(my_y + d, NY) for d in range(NY)]
    z_at = [lax.rem(my_z + d, NZ) for d in range(NZ)]
    along_z = [{"shard": my_y * NZ + z_at[d]} for d in range(NZ)]
    along_y = [{"shard": y_at[d] * NZ + my_z} for d in range(NY)]
    far_first = (4, 3, 5, 2, 6, 1, 7)

    barrier = pltpu.get_barrier_semaphore()
    for peer in [along_z[d] for d in far_first] + [along_y[d] for d in (2, 1, 3)] + [sibling]:
        pl.semaphore_signal(barrier, inc=1, device_id=peer, device_id_type=MESH)

    load_memory = pltpu.make_async_copy(mem_hbm, mem_ref.at[my_y], mem_sem)
    load_memory.start()

    row = lax.broadcasted_iota(I32, (8, 64), 0)
    label = jnp.zeros((8, 64), I32)
    for i in range(8):
        label = jnp.where(row == i, lab_ref[i], label)
    tab_ref[:, 0:64] = jnp.where(mask_ref[...] > 0, id_ref[...], -1)
    tab_ref[:, 64:128] = label
    half_ref[...] = tab_ref[...].astype(I16)
    qall[my_z] = q_ref[...]
    tall[my_z] = half_ref[...]
    labs[my_y] = mlab_ref[...]

    def put(src, dst, send, recv, peer):
        pltpu.make_async_remote_copy(
            src_ref=src, dst_ref=dst, send_sem=send_sem.at[send], recv_sem=recv_sem.at[recv],
            device_id=peer, device_id_type=MESH,
        ).start()

    def await_bytes(sem, index, view):
        pltpu.make_async_copy(view, view, sem.at[index]).wait()

    def await_line(recv, buf):
        await_bytes(recv_sem, recv, buf.at[pl.ds(0, NZ - 1)])

    def to_line(src, dst, send, recv):
        for d in far_first:
            put(src.at[z_at[d]], dst.at[my_z], send, recv, along_z[d])

    def on_line(src, dst, send, recv):
        for d in far_first:
            put(src, dst.at[my_z], send, recv, along_z[d])

    def part(piece):
        return pl.ds(pl.multiple_of(core * (block_rows // 2) + piece * 128, 128), 128)

    def hand_on(block, piece, recv):
        view = mem_ref.at[block, part(piece)]
        put(view, view, S_MEM, recv, sibling)

    pl.semaphore_wait(barrier, NZ + NY - 1)
    on_line(half_ref, tall, S_TAB, TAB)
    on_line(q_ref, qall, S_IN, IN)
    for up_piece, down_piece in ((0, 2), (1, 3), (2, 0), (3, 1)):
        for piece, recv, peer in ((up_piece, DOWN, along_y[1]), (down_piece, UP, along_y[3])):
            put(mem_hbm.at[part(piece)], mem_ref.at[my_y, part(piece)], S_MEM, recv + piece, peer)
    for d in (2, 1, 3):
        put(mlab_ref, labs.at[my_y], S_LAB, LAB, along_y[d])

    def landed(block, piece, recv):
        await_bytes(recv_sem, recv + piece, mem_ref.at[block, part(piece)])

    for step in range(2):
        piece = step
        landed(y_at[3], piece, DOWN)
        view = mem_ref.at[y_at[3], part(piece)]
        put(view, view, S_MEM, RELAY + piece, along_y[1])
        hand_on(y_at[3], piece, SIB)
        piece = step + 2
        landed(y_at[1], piece, UP)
        view = mem_ref.at[y_at[1], part(piece)]
        put(view, view, S_MEM, RELAY + piece, along_y[3])
        hand_on(y_at[1], piece, SIB + 1)

    await_line(TAB, tall)
    lane = lax.broadcasted_iota(I32, (8, 128), 1)
    for i in range(NZ):
        idall[i] = tall[i].astype(I32)

    def invert(b, y):
        local = idall[b] - (y * NZ + my_z) * block_rows
        found = [jnp.full((8, 128), -1, I32) for _ in range(nb)]
        for k in range(64):
            here = jnp.broadcast_to(local[:, k : k + 1], (8, 128))
            for a in range(nb):
                found[a] = jnp.where(here == lane + a * 128, 64 + k, found[a])
        for a in range(nb):
            inv_ref[b, y * nb + a] = found[a]
        return y

    def invert_owner(b):
        def one(y, c):
            invert(b, y)
            return c

        lax.fori_loop(0, NY, one, 0)

    owner = iter(range(NZ))
    for step in range(2):
        piece = step + 2
        landed(y_at[3], piece, DOWN)
        hand_on(y_at[3], piece, SIB)
        invert_owner(next(owner))
        piece = step
        landed(y_at[1], piece, UP)
        hand_on(y_at[1], piece, SIB + 1)
        invert_owner(next(owner))
    for piece in (0, 2, 1, 3):
        landed(y_at[2], piece, RELAY)
        hand_on(y_at[2], piece, SIB + 2)
        if piece in EARLY:
            invert_owner(next(owner))

    await_line(IN, qall)
    load_memory.wait()
    queries = jnp.concatenate([qall[i].astype(F32) for i in range(NZ)], axis=0).astype(BF16)
    for step, (d, arrived) in enumerate(((0, None), (3, SIB), (1, SIB + 1), (2, SIB + 2))):
        y = y_at[d]
        if arrived is not None:
            await_bytes(recv_sem, arrived, mem_ref.at[y, pl.ds(0, block_rows // 2)])
        s_ref[...] = dot_nt(queries, mem_ref[y])
        for i in range(NZ // 2):
            pair = None
            for j in (i, i + NZ // 2):
                local = idall[j] - (y * NZ + my_z) * block_rows
                place = jnp.bitwise_and(local, 127)
                which = jnp.right_shift(local, 7)
                value = jnp.zeros((8, 128), F32)
                for a in range(nb):
                    block = s_ref[j * 8 : j * 8 + 8, a * 128 : a * 128 + 128]
                    value = jnp.where(which == a, lane_gather(block, place), value)
                value = jnp.where(lane < 64, value * HALF_INV_TAU, 0.0)
                pair = value if pair is None else pair + pltpu.roll(value, 64, axis=1)
            ppart[i] = pair if step == 0 else ppart[i] + pair
    on_line(ppart, pz, S_POS, POS)
    pz[my_z] = ppart[...]

    for _ in range(3):
        invert_owner(next(owner))
    await_bytes(recv_sem, LAB, labs.at[pl.ds(0, NY - 1)])
    queries = jnp.concatenate([queries, queries], axis=0)
    ids = idall[...].reshape(NZ * 8, 128)
    labels = jnp.transpose(jnp.concatenate([ids, ids], axis=0))[64:65, :]

    def score(y, c):
        lab_t = columns(labs[y])
        for a in range(nb):
            st = dot_nt(mem_ref[y, a * 128 : a * 128 + 128, :], queries) * HALF_INV_TAU
            column = jnp.broadcast_to(lab_t[:, a : a + 1], (128, 128))
            st_ref[pl.ds(pl.multiple_of(y * block_rows + a * 128, 128), 128), :] = jnp.where(
                column != labels, st, FAR
            )
            flipped = jnp.transpose(mem_ref[y, a * 128 : a * 128 + 128, :].astype(F32))
            memt_ref[:, pl.ds(pl.multiple_of(y * block_rows + a * 128, 128), 128)] = flipped.astype(BF16)
        return c

    lax.fori_loop(0, NY, score, 0)

    await_line(POS, pz)
    pos = jnp.sum(pz[...], axis=0)
    half_line = NZ // 2
    own = jnp.where(lane < 64, pos[0], 0.0)
    for i in range(1, NZ):
        block = pos[i % half_line]
        block = pltpu.roll(block, 64, axis=1) if i >= half_line else block
        own = jnp.where(jnp.logical_and(my_z == i, lane < 64), block, own)
    pos = pos.reshape(half_line * 8, 128)
    pt_ref[...] = twice(jnp.concatenate([pos, pltpu.roll(pos, 64, axis=1)], axis=0))[:32, :]
    zero = jnp.zeros((8, 128), F32)
    mask = jnp.where(jnp.logical_and(lane < 64, tab_ref[...] >= 0), 1.0, 0.0)
    found = jnp.sum(mask, axis=1, keepdims=True)

    def first_pass(c):
        p = [jnp.broadcast_to(pt_ref[c * KB + i : c * KB + i + 1, :], (8, 128)) for i in range(KB)]

        def step(g, acc):
            acc = list(acc)
            at = [pl.ds(pl.multiple_of(g * (8 * G), 8 * G) + 8 * v, 8) for v in range(G)]
            for i in range(KB):
                one = two = None
                for v in range(G):
                    t = jnp.tanh(st_ref[at[v], :] - p[i])
                    tt = t * t
                    if c:
                        squares[(c - 1) * KB + i, at[v], :] = tt
                    one = t if one is None else one + t
                    two = tt if two is None else two + tt
                acc[2 * i] = acc[2 * i] + (one + float(G))
                acc[2 * i + 1] = acc[2 * i + 1] + (float(G) - two)
            return tuple(acc)

        acc = lax.fori_loop(0, rows // (8 * G), step, (zero,) * (2 * KB), unroll=4)
        for i in range(KB):
            racc[i] = acc[2 * i]
            racc[KB + i] = acc[2 * i + 1]
        sums = jnp.sum(racc[...], axis=1)
        spread = [jnp.zeros((8, 128), F32)] * 16
        spread[c] = 0.5 * sums[:KB, :]
        spread[8 + c] = 0.25 * sums[KB:, :]
        both = jnp.transpose(jnp.concatenate(spread, axis=0))
        both = both[:64, :] + pltpu.roll(both[64:, :], 32, axis=1)
        rpart[c] = both.reshape(NZ, 8, 128)
        to_line(rpart.at[c], rrs.at[c], S_RANK, RANK + c)
        rrs[c, my_z] = rpart[c, my_z]

    def positive_terms():
        own_t = columns(own)
        mask_t = columns(mask)
        off = jnp.where(
            lax.broadcasted_iota(I32, (64, 128), 0) == lax.broadcasted_iota(I32, (64, 128), 1),
            0.0, 1.0,
        )
        for i in range(8):
            col = jnp.broadcast_to(own_t[:64, i : i + 1], (64, 128))
            mcol = jnp.broadcast_to(mask_t[:64, i : i + 1], (64, 128)) * off
            t = jnp.tanh(col - own[i : i + 1, :])
            w = (1.0 - t * t) * (0.25 * off)
            wq_ref[i] = w
            aux_ref[i : i + 1, :] = 1.0 + jnp.sum(mcol * (0.5 + 0.5 * t), axis=0, keepdims=True)
            aux_ref[8 + i : 9 + i, :] = jnp.sum(mcol * w, axis=0, keepdims=True)

    def owner_terms(c):
        await_line(RANK + c, rrs.at[c])
        rank_neg = jnp.sum(rrs[c], axis=0)
        if c:
            rank_neg = rank_neg + ranks[...]
        ranks[...] = rank_neg
        rank_pos = aux_ref[0:8, :]
        total = rank_pos + rank_neg
        share = mask / (found * total * total)
        weight_neg = share * rank_pos
        both = jnp.where(lane < 64, weight_neg * (0.5 * HALF_INV_TAU), 0.0)
        if c == NK - 1:
            slope_neg = pltpu.roll(rank_neg, 64, axis=1)
            spread = aux_ref[8:16, :]
            weight_pos = -share * rank_neg
            wp_t = columns(weight_pos)
            for i in range(8):
                col = jnp.broadcast_to(wp_t[:64, i : i + 1], (64, 128))
                aux_ref[16 + i : 17 + i, :] = jnp.sum(col * wq_ref[i], axis=0, keepdims=True)
            backed = aux_ref[16:24, :]
            dpos = mask * backed - weight_neg * slope_neg - weight_pos * spread
            dpos = pltpu.roll(dpos * (2.0 * HALF_INV_TAU), 64, axis=1)
            both = jnp.where(lane < 64, both, dpos)
        wdown[c] = both
        on_line(wdown.at[c], wdall.at[c], S_WEIGHT, WEIGHT + c)
        wdall[c, my_z] = both
        if c == NK - 1:
            precision = jnp.sum(mask * rank_pos / total, axis=1, keepdims=True) / found
            for i in range(8):
                prec_ref[i] = precision[i, 0]

    def weigh(c, at, acc):
        for i in range(KB):
            w = jnp.broadcast_to(wt_ref[c * KB + i : c * KB + i + 1, :], (8, 128))
            if not c:
                p = jnp.broadcast_to(pt_ref[i : i + 1, :], (8, 128))
            for v in range(len(at)):
                if c:
                    tt = squares[(c - 1) * KB + i, at[v], :]
                else:
                    t = jnp.tanh(st_ref[at[v], :] - p)
                    tt = t * t
                acc[v] = acc[v] + w * (1.0 - tt)
        return acc

    def await_weights(c):
        await_line(WEIGHT + c, wdall.at[c])
        weights = twice(wdall[c].reshape(NZ * 8, 128))
        wt_ref[c * KB : c * KB + KB, :] = weights[c * KB : c * KB + KB, :]

    def second_pass(c):
        await_weights(c)

        def block(jb, carry):
            start = pl.multiple_of(jb * (8 * JC), 8 * JC)
            at = [pl.ds(start + 8 * v, 8) for v in range(JC)]
            acc = weigh(c, at, [ct_ref[at[v], :] if c else zero for v in range(JC)])
            for v in range(JC):
                ct_ref[at[v], :] = acc[v]
            return carry

        lax.fori_loop(0, rows // (8 * JC), block, 0, unroll=2)

    def last_pass(c):
        await_weights(c)
        def block(a, carry):
            start = pl.multiple_of(a * 128, 128)
            at = [pl.ds(start + 8 * v, 8) for v in range(16)]
            acc = weigh(c, at, [ct_ref[at[v], :] for v in range(16)])
            neg = jnp.concatenate(acc, axis=0)
            top = neg.astype(BF16)
            cneg_ref[pl.ds(start, 128), 0:128] = top
            cneg_ref[pl.ds(start, 128), 128:256] = (neg - top.astype(F32)).astype(BF16)
            pos = []
            for i in range(NZ):
                index = inv_ref[i, a]
                value = lane_gather(wdall[c, i], jnp.bitwise_and(index, 127))
                pos.append(jnp.where(index >= 0, value, 0.0))
            pos = jnp.concatenate(pos, axis=0)
            top = pos.astype(BF16)
            cpos_ref[0:64, pl.ds(start, 128)] = top
            cpos_ref[64:128, pl.ds(start, 128)] = (pos - top.astype(F32)).astype(BF16)
            return carry

        lax.fori_loop(0, rows // 128, block, 0, unroll=8)
        neg = pos = None
        for y in range(NY):
            span = slice(y * block_rows, (y + 1) * block_rows)
            one = dot_nn(memt_ref[:, span], cneg_ref[span, :])
            two = dot_nn(cpos_ref[:, span], mem_ref[y])
            neg = one if neg is None else neg + one
            pos = two if pos is None else pos + two
        neg = jnp.transpose(neg[:, :128] + neg[:, 128:])
        grad = neg[:64, :] + neg[64:, :] + pos[:64, :] + pos[64:, :]
        gpart[...] = grad.reshape(NZ, 8, width)
        to_line(gpart, grs, S_GRAD, GRAD)
        grs[my_z] = gpart[my_z]

    first_pass(0)
    first_pass(1)
    positive_terms()
    first_pass(2)
    owner_terms(0)
    first_pass(3)
    owner_terms(1)
    for b in owner:
        invert_owner(b)
    owner_terms(2)
    second_pass(0)
    owner_terms(3)
    second_pass(1)
    second_pass(2)
    last_pass(3)

    await_line(GRAD, grs)
    grad_ref[...] = jnp.sum(grs[...], axis=0)
    await_bytes(send_sem, S_MEM, mem_ref.at[pl.ds(0, 3)])
    await_bytes(send_sem, S_LAB, labs.at[pl.ds(0, NY - 1)])
    for send, buf in ((S_IN, qall), (S_TAB, tall), (S_POS, pz), (S_GRAD, grs)):
        await_bytes(send_sem, send, buf.at[pl.ds(0, NZ - 1)])
    for c in range(NK):
        await_bytes(send_sem, S_RANK, rrs.at[c, pl.ds(0, NZ - 1)])
        await_bytes(send_sem, S_WEIGHT, wdall.at[c, pl.ds(0, NZ - 1)])


def hand_over(prec_in, grad_in, prec_out, grad_out):
    for i in range(8):
        prec_out[i] = prec_in[i]
    grad_out[...] = grad_in[...]


def on_device(queries, query_labels, positive_ids, positive_mask, memory, memory_labels):
    own, width = queries.shape
    rows = memory.shape[0]
    vmem = pl.BlockSpec(memory_space=pltpu.VMEM)
    smem = pl.BlockSpec(memory_space=pltpu.SMEM)
    precision, grad = pl.pallas_call(
        kernel,
        out_shape=(
            jax.ShapeDtypeStruct((own,), F32),
            jax.ShapeDtypeStruct((own, width), F32),
        ),
        in_specs=[smem, vmem, vmem, vmem, vmem, pl.BlockSpec(memory_space=pltpu.HBM)],
        out_specs=(smem, vmem),
        scratch_shapes=[
            pltpu.VMEM((NY, rows, width), BF16),
            pltpu.VMEM((NY, rows // 128, 128), I32),
            pltpu.VMEM((own, 128), I32),
            pltpu.VMEM((own, 128), I16),
            pltpu.VMEM((NZ, own, width), BF16),
            pltpu.VMEM((NZ, own, 128), I16),
            pltpu.VMEM((NZ, own, 128), I32),
            pltpu.VMEM((NZ * own, rows), F32),
            pltpu.VMEM((NY * rows, 128), F32),
            pltpu.VMEM((NZ, NY * rows // 128, own, 128), I32),
            pltpu.VMEM((NY * rows, 128), F32),
            pltpu.VMEM((NZ // 2, own, 128), F32),
            pltpu.VMEM((NZ, NZ // 2, own, 128), F32),
            pltpu.VMEM((32, 128), F32),
            pltpu.VMEM((own, 64, 128), F32),
            pltpu.VMEM((24, 128), F32),
            pltpu.VMEM((2 * KB, 8, 128), F32),
            pltpu.VMEM(((NK - 1) * KB, NY * rows, 128), F32),
            pltpu.VMEM((NK, NZ, own, 128), F32),
            pltpu.VMEM((NK, NZ, own, 128), F32),
            pltpu.VMEM((own, 128), F32),
            pltpu.VMEM((NK, own, 128), F32),
            pltpu.VMEM((NK, NZ, own, 128), F32),
            pltpu.VMEM((32, 128), F32),
            pltpu.VMEM((width, NY * rows), BF16),
            pltpu.VMEM((NY * rows, 256), BF16),
            pltpu.VMEM((128, NY * rows), BF16),
            pltpu.VMEM((NZ, own, width), F32),
            pltpu.VMEM((NZ, own, width), F32),
            pltpu.SemaphoreType.DMA((N_SEND,)),
            pltpu.SemaphoreType.DMA((N_RECV,)),
            pltpu.SemaphoreType.DMA,
        ],
        compiler_params=pltpu.CompilerParams(
            collective_id=0, has_side_effects=True, vmem_limit_bytes=VMEM_LIMIT
        ),
    )(
        query_labels, queries, positive_ids, positive_mask,
        memory_labels.reshape(rows // 128, 128), memory,
    )
    return pl.pallas_call(
        hand_over,
        out_shape=(
            jax.ShapeDtypeStruct((own,), F32),
            jax.ShapeDtypeStruct((own, width), F32),
        ),
        in_specs=[smem, vmem],
        out_specs=(smem, vmem),
    )(precision, grad)


def solution(mesh):
    return jax.shard_map(
        on_device,
        mesh=mesh,
        in_specs=(
            P(("dp", "shard"), None),
            P(("dp", "shard")),
            P(("dp", "shard"), None),
            P(("dp", "shard"), None),
            P("shard", None),
            P("shard"),
        ),
        out_specs=(P(("dp", "shard")), P(("dp", "shard"), None)),
        check_vma=False,
    )
```
